32 devices in a mesh: dp: 16 (over z, y, x), tensor: 2 (over core).
Axes of the slice: x: 2, y: 2, z: 4, core: 2. Of those that a mesh axis runs over, the one named last changes fastest.
Arguments:
- hidden: bfloat16 [32, 512, 768], P('dp'), as said below
- lengths: int32 [32], P('dp'), may hold values from 64 to 512, as said below
- spans: int32 [32, 512], P('dp'), may hold values from 0 to 511, as said below
- join_query: float32 [768], replicated, as said below
- w_qkv: bfloat16 [768, 3, 768], P(None, None, 'tensor'), as said below
- qv_bias: float32 [2, 768], P(None, 'tensor'), may hold values from -3 to 3
- w_out: bfloat16 [768, 768], P(None, 'tensor'), as said below
- out_biases: float32 [2, 768], replicated, may hold values from -2 to 2
- norm_gains: float32 [2, 768], replicated, may hold values from 0.5 to 1.5
- norm_biases: float32 [2, 768], replicated, may hold values from -2 to 2
- w_up: bfloat16 [768, 3072], P(None, 'tensor'), as said below
- up_bias: float32 [3072], P('tensor'), may hold values from -3 to 3
- w_down: bfloat16 [768, 3072], P(None, 'tensor'), as said below
- cotangent: bfloat16 [32, 512, 768], P('dp'), may hold values from -6 to 6
Outputs:
- layer_out: bfloat16 [32, 512, 768], P('dp')
- grad_hidden: float32 [32, 512, 768], P('dp')
- grad_qkv: float32 [768, 3, 768], P('dp', None, 'tensor')
- grad_qv_bias: float32 [2, 768], P(None, 'tensor')
- grad_out_proj: float32 [768, 768], P('dp', 'tensor')
- grad_out_biases: float32 [2, 768], replicated
- grad_norm_gains: float32 [2, 768], replicated
- grad_norm_biases: float32 [2, 768], replicated
- grad_up: float32 [768, 3072], P('dp', 'tensor')
- grad_up_bias: float32 [3072], P('tensor')
- grad_down: float32 [768, 3072], P('dp', 'tensor')
- grad_join_query: float32 [768], replicated
The draws below stay inside these ranges and needn't reach their ends.
Inputs may be any that keep to these rules, and one draw needn't show every extreme that they name: `lengths`: each row's pad mask marks its positions at or beyond its length; some row has length 512. `spans`: along a row the ids start at 0 and rise by 0 or 1 from one position to the next; a new span starts at the row's length; in some row every position is a span of its own. `hidden`: independent entries of mean 0 and deviation 1. `join_query`: independent entries of mean 0 and deviation 2 / sqrt(768). `w_qkv`: independent entries of mean 0 and deviation 1 / sqrt(768). `w_out`: independent entries of mean 0 and deviation 4 / sqrt(768). `w_up`: independent entries of mean 0 and deviation 1 / sqrt(768). `w_down`: independent entries of mean 0 and deviation 1 / sqrt(3072).
All inputs are finite; a program needn't handle non-finite values.
Results may differ from the reference program's by a relative error of at most 0.012.
The reference program's roundings to bfloat16 on the way count: a program that leaves them out, or rounds other values in their place, can miss the bound.
Values sent between devices are 32-bit elements; how exact they have to be, the bound alone decides.
No kernel may reach another device: no remote copies, remote signals or barrier semaphores. Data moves between devices by JAX's collectives and lax.ppermute only.
A program may use at most 192 MiB of HBM per device.

```python
import math
import jax
import jax.numpy as jnp
from jax import lax

D = 768
HEADS = 12
HEAD = 64
FF = 3072
LEN = 512
MINLEN = 64
ROWS = 32


def row_lengths(key):
    drawn = jax.random.randint(jax.random.fold_in(key, 17), (ROWS,), MINLEN, LEN + 1)
    return drawn.at[0].set(LEN).astype(jnp.int32)


def draw_lengths(key, part):
    return row_lengths(key)


def draw_spans(key, part):
    row_lens = row_lengths(key)
    starts = jax.random.randint(jax.random.fold_in(key, 29), (ROWS, LEN), 0, 4) == 0
    places = jnp.arange(LEN, dtype=jnp.int32)[None, :]
    last_row = jnp.arange(ROWS, dtype=jnp.int32)[:, None] == ROWS - 1
    starts = starts | (places == row_lens[:, None]) | (places == 0) | last_row
    return (jnp.cumsum(starts.astype(jnp.int32), axis=1) - 1).astype(jnp.int32)


def drawn_field(key, shape, deviation):
    values = jnp.clip(jax.random.normal(jax.random.fold_in(key, 43), shape, jnp.float32), -4.0, 4.0)
    return values * deviation


def draw_hidden(key, part):
    return drawn_field(key, (ROWS, LEN, D), 1.0).astype(jnp.bfloat16)


def draw_join_query(key, part):
    return drawn_field(key, (D,), 2.0 / math.sqrt(D))


def draw_w_qkv(key, part):
    return drawn_field(key, (D, 3, D), 1.0 / math.sqrt(D)).astype(jnp.bfloat16)


def draw_w_out(key, part):
    return drawn_field(key, (D, D), 4.0 / math.sqrt(D)).astype(jnp.bfloat16)


def draw_w_up(key, part):
    return drawn_field(key, (D, FF), 1.0 / math.sqrt(D)).astype(jnp.bfloat16)


def draw_w_down(key, part):
    return drawn_field(key, (D, FF), 1.0 / math.sqrt(FF)).astype(jnp.bfloat16)


def raised(values, key, source, target, shards_of, factor):
    def block_of(dim):
        return (jnp.arange(values.shape[dim]) // (values.shape[dim] // shards_of)).reshape((-1,) + (1,) * (values.ndim - 1 - dim))

    one_side = jax.random.permutation(key, shards_of)[block_of(target)]
    second = (block_of(target) + shards_of // 2) % shards_of
    return jnp.where((block_of(source) == one_side) | (block_of(source) == second), factor * values, values)


def block_levels(own_key, extent, shards, smallest, top_value):
    factor_of, own = 1.0, jax.random.fold_in(own_key, 6)
    for position, blocks in shards:
        steps = jnp.exp(jax.random.uniform(jax.random.fold_in(own, position), (blocks,), jnp.float32, smallest / len(shards), top_value / len(shards)))
        factor_of = factor_of * jnp.repeat(steps, extent[position] // blocks).reshape([-1 if axis == position else 1 for axis in range(len(extent))])
    return factor_of


def scatter_about(key, shape, width, bound, split=(), kind=jnp.bfloat16):
    level = block_levels(key, shape, split, -0.22, 0.18) if split else 1.0
    array = jax.random.normal(key, shape, jnp.float32) * width * level
    return jnp.minimum(jnp.maximum(array, -bound), bound).astype(kind)


def heavy_noise(rng, shape, scale, most, split, heavy, kind=jnp.bfloat16):
    array = scale * jax.random.normal(rng, shape, jnp.float32)
    if split:
        array = array * block_levels(rng, shape, split, -0.22, 0.18)
    return jnp.clip(raised(array, jax.random.fold_in(rng, 3), *heavy), -most, most).astype(kind)


def setup_inputs(seed: int = 0) -> dict:
    key_list = jax.random.split(jax.random.key(seed), 15)
    hidden = draw_hidden(jax.random.fold_in(key_list[14], 71), 0)
    lengths = draw_lengths(jax.random.fold_in(key_list[14], 71), 0)
    spans = draw_spans(jax.random.fold_in(key_list[14], 71), 0)
    join_query = draw_join_query(jax.random.fold_in(key_list[14], 71), 0)
    w_qkv = draw_w_qkv(jax.random.fold_in(key_list[14], 71), 0)
    qv_bias = scatter_about(key_list[5], (2, D), 0.5, 3.0, ((1, 2),), jnp.float32)
    w_out = draw_w_out(jax.random.fold_in(key_list[14], 71), 0)
    out_biases = scatter_about(key_list[7], (2, D), 0.3, 2.0, (), jnp.float32)
    norm_gains = jnp.clip(1.0 + 0.1 * jax.random.normal(key_list[8], (2, D), jnp.float32), 0.5, 1.5)
    norm_biases = scatter_about(key_list[9], (2, D), 0.3, 2.0, (), jnp.float32)
    w_up = draw_w_up(jax.random.fold_in(key_list[14], 71), 0)
    up_bias = scatter_about(key_list[11], (FF,), 0.5, 3.0, ((0, 2),), jnp.float32)
    w_down = draw_w_down(jax.random.fold_in(key_list[14], 71), 0)
    cotangent = heavy_noise(key_list[13], (ROWS, LEN, D), 1.0, 6.0, ((0, 16),), (0, 2, 16, 2.0))
    return dict(hidden=hidden, lengths=lengths, spans=spans, join_query=join_query, w_qkv=w_qkv, qv_bias=qv_bias, w_out=w_out, out_biases=out_biases, norm_gains=norm_gains, norm_biases=norm_biases, w_up=w_up, up_bias=up_bias, w_down=w_down, cotangent=cotangent)


HIGH = lax.Precision.HIGHEST
EPS = 1e-05
NEGATIVE = -1e+30

@jax.custom_vjp
def low(v):
    return lax.optimization_barrier(v.astype(jnp.bfloat16)).astype(jnp.float32)

@jax.custom_vjp
def low_back(v):
    return v

def low_keep(v):
    return (low(v), None)

def low_pass(kept, grad):
    return (grad,)

def back_keep(v):
    return (v, None)

def back_low(kept, grad):
    return (low(grad),)
low.defvjp(low_keep, low_pass)
low_back.defvjp(back_keep, back_low)

def norm_apply(resid, gain_vec, shift_vec):
    row_mean = lax.optimization_barrier(jnp.mean(resid, -1, keepdims=True))
    centered = resid - row_mean
    variance = lax.optimization_barrier(jnp.mean(centered * centered, -1, keepdims=True))
    return centered * lax.rsqrt(variance + EPS) * gain_vec + shift_vec

def layer_rows(inputs_f, lens_grp, spans_grp, params):
    join_query, w_qkv, qv_bias, w_out, out_biases, norm_gains, norm_biases, w_up, up_bias, w_down = params
    seq_len = inputs_f.shape[1]
    is_valid = jnp.arange(seq_len, dtype=jnp.int32)[None, :] < lens_grp[:, None]
    same_mask = spans_grp[:, :, None] == spans_grp[:, None, :]
    same_span = same_mask.astype(jnp.float32)
    joining_score = jnp.einsum('gld,d->gl', inputs_f, join_query, precision=HIGH)
    span_top = lax.optimization_barrier(jnp.max(jnp.where(same_mask, joining_score[:, None, :], NEGATIVE), axis=2))
    weight = jnp.exp(joining_score - span_top)
    numerator = jnp.einsum('gij,gjd->gid', same_span, weight[..., None] * inputs_f, precision=HIGH)
    denominator = jnp.einsum('gij,gj->gi', same_span, weight, precision=HIGH)
    joined_in = inputs_f + numerator / denominator[..., None]
    joined_low = low(joined_in)
    projected = low_back(jnp.einsum('gld,dcf->glcf', joined_low, w_qkv, precision=HIGH))
    head_shape = projected.shape[:2] + (HEADS, HEAD)
    query_vec = low(projected[:, :, 0] + qv_bias[0]).reshape(head_shape)
    key_vec = low(projected[:, :, 1]).reshape(head_shape)
    value_vec = low(projected[:, :, 2] + qv_bias[1]).reshape(head_shape)
    scale = 1.0 / math.sqrt(HEAD)
    scores = low_back(jnp.einsum('gqhe,gkhe->ghqk', query_vec, key_vec, precision=HIGH) * scale)
    scores = jnp.where(is_valid[:, None, None, :], scores, NEGATIVE)
    row_max = lax.optimization_barrier(jnp.max(scores, -1, keepdims=True))
    expo = jnp.exp(scores - row_max)
    attn_probs = low(expo / lax.optimization_barrier(jnp.sum(expo, -1, keepdims=True)))
    context = jnp.einsum('ghqk,gkhe->gqhe', attn_probs, value_vec, precision=HIGH).reshape(joined_in.shape)
    context = low(low_back(context))
    attn_out = low_back(jnp.einsum('gli,oi->glo', context, w_out, precision=HIGH)) + out_biases[0]
    first_norm = norm_apply(joined_in + attn_out, norm_gains[0], norm_biases[0])
    up_proj = low_back(jnp.einsum('gld,df->glf', low(first_norm), w_up, precision=HIGH)) + up_bias
    activated = low(jax.nn.gelu(up_proj, approximate=False))
    down_out = low_back(jnp.einsum('glf,of->glo', activated, w_down, precision=HIGH)) + out_biases[1]
    return norm_apply(first_norm + down_out, norm_gains[1], norm_biases[1])

def reference(hidden, lengths, spans, join_query, w_qkv, qv_bias, w_out, out_biases, norm_gains, norm_biases, w_up, up_bias, w_down, cotangent):
    inputs_f = hidden.astype(jnp.float32)
    row_total = inputs_f.shape[0]
    seq_len = inputs_f.shape[1]
    model_width = inputs_f.shape[2]
    group = math.gcd(row_total, 8)
    n_groups = row_total // group
    params = (join_query, w_qkv.astype(jnp.float32), qv_bias, w_out.astype(jnp.float32), out_biases, norm_gains, norm_biases, w_up.astype(jnp.float32), up_bias, w_down.astype(jnp.float32))

    def forward(inputs_all, params_all):

        def one_group(pieces):
            return layer_rows(pieces[0], pieces[1], pieces[2], params_all)
        grouped = lax.map(jax.checkpoint(one_group), (inputs_all.reshape(n_groups, group, seq_len, model_width), lengths.reshape(n_groups, group), spans.reshape(n_groups, group, seq_len)))
        return grouped.reshape(inputs_all.shape)
    outputs, pull_back = jax.vjp(forward, inputs_f, params)
    is_valid = (jnp.arange(seq_len, dtype=jnp.int32)[None, :] < lengths[:, None]).astype(jnp.float32)
    d_out = cotangent.astype(jnp.float32) * is_valid[..., None]
    grad_inputs, grads = pull_back(d_out)
    g_join, g_qkv, g_qvb, g_out, g_outb, g_gains, g_nbias, g_up, g_upb, g_down = grads
    return (outputs.astype(jnp.bfloat16), grad_inputs, g_qkv, g_qvb, g_out, g_outb, g_gains, g_nbias, g_up, g_upb, g_down, g_join)
```

```python
import functools
import math

import jax
import jax.numpy as jnp
from jax import lax
from jax.experimental import pallas as pl
from jax.experimental.pallas import tpu as pltpu
from jax.sharding import PartitionSpec as P

HEAD = 64


HIGH = lax.Precision.HIGHEST
EPS = 1e-05
NEGATIVE = -1e30
CONTRACT_LAST = (((1,), (1,)), ((), ()))
CONTRACT_FIRST = (((0,), (0,)), ((), ()))
VMEM_LIMIT = 50 * 1024 * 1024


def swap_cores(part):
    return lax.ppermute(part, "tensor", [(0, 1), (1, 0)])


STEP_X, STEP_Y, STEP_Z, STEP_W = 1, 2, 4, 12
ORDERS = (
    (STEP_X, STEP_Y, STEP_Z, STEP_W),
    (STEP_Y, STEP_X, STEP_Z, STEP_W),
    (STEP_Z, STEP_W, STEP_X, STEP_Y),
)


def relative_block(order, place):
    steps = len(order)
    block = 0
    for position, mask in enumerate(order):
        if (place >> (steps - 1 - position)) & 1:
            block ^= mask
    return block


def grad_kernel(parts, rows, *refs):
    here_ref = refs[0]
    operands = refs[1 : 1 + 2 * len(parts)]
    outs = refs[1 + 2 * len(parts) : 1 + 2 * len(parts) + 6]
    totals = refs[1 + 2 * len(parts) + 6 : -1]
    sem = refs[-1]
    here = here_ref[0]
    copies = []
    slot = 0
    for colour, order in enumerate(ORDERS):
        column = 0
        for part, ranges in enumerate(parts):
            start, width = ranges[colour]
            if width == 0:
                continue
            total = totals[slot]
            slot += 1
            total[...] = lax.dot_general(
                operands[2 * part][...],
                operands[2 * part + 1][:, start : start + width],
                CONTRACT_FIRST,
                preferred_element_type=jnp.float32,
            )
            for place in range(16):
                block = jnp.bitwise_xor(here, relative_block(order, place))
                source = total.at[pl.ds(pl.multiple_of(block * rows, 8), rows), :]
                target = outs[2 * colour + place // 8].at[place % 8, :, pl.ds(column, width)]
                copy = pltpu.make_async_copy(source, target, sem.at[colour])
                copy.start()
                copies.append((copy, colour))
            column += width
    for copy, colour in copies:
        copy.wait()


def grad_blocks(here, operands, parts):
    tokens, height = operands[0][0].shape
    rows = height // 16
    widths = [sum(ranges[colour][1] for ranges in parts) for colour in range(3)]
    out_shape = []
    for width in widths:
        out_shape += [jax.ShapeDtypeStruct((8, rows, width), jnp.float32)] * 2
    scratch = []
    for colour in range(3):
        for ranges in parts:
            if ranges[colour][1]:
                scratch.append(pltpu.VMEM((height, ranges[colour][1]), jnp.float32))
    flops = sum(2 * tokens * height * right.shape[1] for _, right in operands)
    moved = sum(left.size * 2 + right.size * 2 + height * right.shape[1] * 4 for left, right in operands)
    outs = pl.pallas_call(
        functools.partial(grad_kernel, parts, rows),
        out_shape=tuple(out_shape),
        in_specs=[pl.BlockSpec(memory_space=pltpu.SMEM)]
        + [pl.BlockSpec(memory_space=pltpu.VMEM)] * (2 * len(operands)),
        out_specs=tuple([pl.BlockSpec(memory_space=pl.ANY)] * 6),
        scratch_shapes=scratch + [pltpu.SemaphoreType.DMA((3,))],
        compiler_params=pltpu.CompilerParams(vmem_limit_bytes=VMEM_LIMIT),
        cost_estimate=pl.CostEstimate(flops=flops, bytes_accessed=moved, transcendentals=0),
        name="weight_grads",
    )(here, *[array for pair in operands for array in pair])
    return outs


def scatter_sum(blocks):
    keeps = [blocks[2 * colour] for colour in range(3)]
    sends = [blocks[2 * colour + 1] for colour in range(3)]
    arrived = [[] for _ in ORDERS]
    half = 8
    for step in range(4):
        incoming = [
            lax.ppermute(sends[colour], "dp", [(i, i ^ order[step]) for i in range(16)])
            for colour, order in enumerate(ORDERS)
        ]
        half //= 2
        for colour in range(3):
            arrived[colour].append(incoming[colour])
            if half:
                total = keeps[colour][half : 2 * half]
                for array in arrived[colour]:
                    total = total + array[half : 2 * half]
                sends[colour] = total
    results = []
    for colour in range(3):
        total = keeps[colour][0]
        for array in arrived[colour]:
            total = total + array[0]
        results.append(total)
    return results


def all_sum(values):
    for mask in (STEP_X, STEP_Y, STEP_Z, STEP_W):
        values = values + lax.ppermute(values, "dp", [(i, i ^ mask) for i in range(16)])
    return values


def layer_norm(resid, gain_vec, shift_vec):
    row_mean = jnp.mean(resid, -1, keepdims=True)
    centered = resid - row_mean
    variance = jnp.mean(centered * centered, -1, keepdims=True)
    inv_std = lax.rsqrt(variance + EPS)
    normed = centered * inv_std
    return (normed * gain_vec + shift_vec, normed, inv_std)


def norm_back(grad_in, gain_vec, normed, inv_std):
    d_normed = grad_in * gain_vec
    return inv_std * (
        d_normed
        - jnp.mean(d_normed, -1, keepdims=True)
        - normed * jnp.mean(d_normed * normed, -1, keepdims=True)
    )


def gelu_exact(values):
    return jax.nn.gelu(values, approximate=False)


def row_scores(query_row, key_row, valid_row):
    scale = 1.0 / math.sqrt(HEAD)
    scores = (
        jnp.einsum("qhe,khe->hqk", query_row, key_row, preferred_element_type=jnp.float32) * scale
    )
    return jnp.where(valid_row[None, None, :], scores, NEGATIVE)


def attend_row(pieces):
    query_row, key_row, value_row, valid_row = pieces
    scores = row_scores(query_row, key_row, valid_row)
    row_max = jnp.max(scores, -1, keepdims=True)
    expo = jnp.exp(scores - row_max)
    row_total = jnp.sum(expo, -1, keepdims=True)
    attn_probs = (expo / row_total).astype(jnp.bfloat16)
    context = jnp.einsum("hqk,khe->qhe", attn_probs, value_row, preferred_element_type=jnp.float32)
    return (context, row_max[..., 0] + jnp.log(row_total[..., 0]))


def attend_back(pieces):
    query_row, key_row, value_row, valid_row, log_total, d_context = pieces
    scale = 1.0 / math.sqrt(HEAD)
    scores = row_scores(query_row, key_row, valid_row)
    probs_full = jnp.exp(scores - log_total[:, :, None])
    attn_probs = probs_full.astype(jnp.bfloat16)
    d_probs = jnp.einsum("qhe,khe->hqk", d_context, value_row, preferred_element_type=jnp.float32)
    d_value = jnp.einsum("hqk,qhe->khe", attn_probs, d_context, preferred_element_type=jnp.float32)
    d_scores = probs_full * (d_probs - jnp.sum(d_probs * probs_full, -1, keepdims=True))
    d_scores_low = d_scores.astype(jnp.bfloat16)
    d_query = (
        jnp.einsum("hqk,khe->qhe", d_scores_low, key_row, preferred_element_type=jnp.float32)
        * scale
    )
    d_key = (
        jnp.einsum("hqk,qhe->khe", d_scores_low, query_row, preferred_element_type=jnp.float32)
        * scale
    )
    return (d_query, d_key, d_value)


def per_device(
    spread,
    hidden,
    lengths,
    spans,
    join_query,
    w_qkv,
    qv_bias,
    w_out,
    out_biases,
    norm_gains,
    norm_biases,
    w_up,
    up_bias,
    w_down,
    cotangent,
):
    row_count, seq_len, model_width = hidden.shape
    token_count = row_count * seq_len
    local_width = w_qkv.shape[2]
    heads_here = local_width // HEAD
    head_shape = (row_count, seq_len, heads_here, HEAD)
    inputs_f = hidden.astype(jnp.float32)
    is_valid = lax.broadcasted_iota(jnp.int32, (row_count, seq_len), 1) < lengths[:, None]
    same_mask = spans[:, :, None] == spans[:, None, :]
    same_span = same_mask.astype(jnp.float32)
    joining_score = jnp.einsum("rld,d->rl", inputs_f, join_query, precision=HIGH)
    span_top = jnp.max(jnp.where(same_mask, joining_score[:, None, :], NEGATIVE), axis=2)
    weight = jnp.exp(joining_score - span_top)
    numerator = jnp.einsum("rij,rjd->rid", same_span, weight[..., None] * inputs_f, precision=HIGH)
    denominator = jnp.einsum("rij,rj->ri", same_span, weight, precision=HIGH)
    pooled = numerator / denominator[..., None]
    joined_in = (inputs_f + pooled).reshape(token_count, model_width)
    joined_low = joined_in.astype(jnp.bfloat16)
    projected = jnp.einsum("nd,dcf->ncf", joined_low, w_qkv, preferred_element_type=jnp.float32)
    query_low = (projected[:, 0] + qv_bias[0]).astype(jnp.bfloat16).reshape(head_shape)
    key_low = projected[:, 1].astype(jnp.bfloat16).reshape(head_shape)
    value_low = (projected[:, 2] + qv_bias[1]).astype(jnp.bfloat16).reshape(head_shape)
    context, log_total = lax.map(attend_row, (query_low, key_low, value_low, is_valid))
    context_low = context.reshape(token_count, local_width).astype(jnp.bfloat16)
    attn_part = lax.dot_general(
        context_low, w_out, CONTRACT_LAST, preferred_element_type=jnp.float32
    )
    attn_out = (attn_part + swap_cores(attn_part)) + out_biases[0]
    first_norm, normed_one, inv_one = layer_norm(
        joined_in + attn_out, norm_gains[0], norm_biases[0]
    )
    first_low = first_norm.astype(jnp.bfloat16)
    up_proj = jnp.dot(first_low, w_up, preferred_element_type=jnp.float32) + up_bias
    activated, gelu_pull = jax.vjp(gelu_exact, up_proj)
    act_low = activated.astype(jnp.bfloat16)
    down_part = lax.dot_general(act_low, w_down, CONTRACT_LAST, preferred_element_type=jnp.float32)
    down_out = (down_part + swap_cores(down_part)) + out_biases[1]
    layer_out, normed_two, inv_two = layer_norm(
        first_norm + down_out, norm_gains[1], norm_biases[1]
    )
    d_out = cotangent.astype(jnp.float32).reshape(token_count, model_width) * is_valid.reshape(
        token_count, 1
    ).astype(jnp.float32)
    gain_two = jnp.sum(d_out * normed_two, 0)
    shift_two = jnp.sum(d_out, 0)
    d_down = norm_back(d_out, norm_gains[1], normed_two, inv_two)
    down_bias_grad = jnp.sum(d_down, 0)
    d_down_low = d_down.astype(jnp.bfloat16)
    d_act = jnp.dot(d_down_low, w_down, preferred_element_type=jnp.float32)
    d_up = gelu_pull(d_act)[0]
    up_bias_grad = jnp.sum(d_up, 0)
    d_up_low = d_up.astype(jnp.bfloat16)
    ffn_back = lax.dot_general(d_up_low, w_up, CONTRACT_LAST, preferred_element_type=jnp.float32)
    d_first = (ffn_back + swap_cores(ffn_back)) + d_down
    gain_one = jnp.sum(d_first * normed_one, 0)
    shift_one = jnp.sum(d_first, 0)
    d_attn = norm_back(d_first, norm_gains[0], normed_one, inv_one)
    attn_bias_grad = jnp.sum(d_attn, 0)
    d_attn_low = d_attn.astype(jnp.bfloat16)
    d_context = (
        jnp.dot(d_attn_low, w_out, preferred_element_type=jnp.float32)
        .astype(jnp.bfloat16)
        .reshape(head_shape)
    )
    d_query, d_key, d_value = lax.map(
        attend_back, (query_low, key_low, value_low, is_valid, log_total, d_context)
    )
    d_query = d_query.reshape(token_count, local_width)
    d_key = d_key.reshape(token_count, local_width)
    d_value = d_value.reshape(token_count, local_width)
    qv_grad = jnp.stack([jnp.sum(d_query, 0), jnp.sum(d_value, 0)])
    d_proj = jnp.stack([d_query, d_key, d_value], axis=1).astype(jnp.bfloat16)
    attn_back = jnp.einsum("ncf,dcf->nd", d_proj, w_qkv, preferred_element_type=jnp.float32)
    d_joined = ((attn_back + swap_cores(attn_back)) + d_attn).reshape(row_count, seq_len, model_width)
    d_numer = d_joined / denominator[..., None]
    d_denom = -jnp.sum(d_joined * pooled, -1) / denominator
    d_weighted = jnp.einsum("rij,rid->rjd", same_span, d_numer, precision=HIGH)
    d_weight = jnp.einsum("rij,ri->rj", same_span, d_denom, precision=HIGH) + jnp.sum(
        d_weighted * inputs_f, -1
    )
    d_score = weight * d_weight
    grad_inputs = d_joined + weight[..., None] * d_weighted + d_score[..., None] * join_query
    join_grad = jnp.einsum("rl,rld->d", d_score, inputs_f, precision=HIGH)
    small = (
        qv_grad,
        up_bias_grad,
        jnp.stack([attn_bias_grad, down_bias_grad]),
        jnp.stack([gain_one, gain_two]),
        jnp.stack([shift_one, shift_two]),
        join_grad,
    )
    d_proj_flat = d_proj.reshape(token_count, 3 * local_width)
    if spread == 16 and model_width % 128 == 0:
        here = lax.axis_index("dp").astype(jnp.int32).reshape(1)
        hidden_width = up_bias.shape[0]
        unit = hidden_width // 12
        down_cols = ((0, 5 * unit), (5 * unit, 4 * unit), (9 * unit, 3 * unit))
        up_cols = ((0, 4 * unit), (4 * unit, 5 * unit), (9 * unit, 3 * unit))
        down_rows = jnp.concatenate(
            scatter_sum(grad_blocks(here, [(d_down_low, act_low)], [down_cols])), axis=1
        )
        up_rows = jnp.concatenate(
            scatter_sum(grad_blocks(here, [(first_low, d_up_low)], [up_cols])), axis=1
        )
        w = local_width
        rest = scatter_sum(
            grad_blocks(
                here,
                [(d_attn_low, context_low), (joined_low, d_proj_flat)],
                [((0, 0), (0, 0), (0, w)), ((0, 5 * w // 3), (5 * w // 3, 4 * w // 3), (0, 0))],
            )
        )
        out_rows = rest[2]
        qkv_rows = jnp.concatenate(rest[:2], axis=1).reshape(-1, 3, w)
        sizes = [math.prod(value.shape) for value in small]
        packed = all_sum(jnp.concatenate([value.reshape(-1) for value in small]).reshape(-1, 128)).reshape(-1)
        summed, offset = [], 0
        for value, size in zip(small, sizes):
            summed.append(packed[offset : offset + size].reshape(value.shape))
            offset += size
    else:
        def first_product(left, right):
            total = lax.dot_general(left, right, CONTRACT_FIRST, preferred_element_type=jnp.float32)
            return lax.psum_scatter(total, "dp", scatter_dimension=0, tiled=True)

        down_rows = first_product(d_down_low, act_low)
        up_rows = first_product(first_low, d_up_low)
        out_rows = first_product(d_attn_low, context_low)
        qkv_rows = first_product(joined_low, d_proj_flat).reshape(-1, 3, local_width)
        summed = lax.psum(small, "dp")
    return (
        layer_out.reshape(row_count, seq_len, model_width).astype(jnp.bfloat16),
        grad_inputs,
        qkv_rows,
        summed[0],
        out_rows,
        summed[2],
        summed[3],
        summed[4],
        up_rows,
        summed[1],
        down_rows,
        summed[5],
    )


def solution(mesh):
    return jax.shard_map(
        functools.partial(per_device, mesh.shape["dp"]),
        mesh=mesh,
        in_specs=(
            P("dp", None, None),
            P("dp"),
            P("dp", None),
            P(),
            P(None, None, "tensor"),
            P(None, "tensor"),
            P(None, "tensor"),
            P(),
            P(),
            P(),
            P(None, "tensor"),
            P("tensor"),
            P(None, "tensor"),
            P("dp", None, None),
        ),
        out_specs=(
            P("dp", None, None),
            P("dp", None, None),
            P("dp", None, "tensor"),
            P(None, "tensor"),
            P("dp", "tensor"),
            P(),
            P(),
            P(),
            P("dp", "tensor"),
            P("tensor"),
            P("dp", "tensor"),
            P(),
        ),
        check_vma=False,
    )
```

```python
import functools
import math

import jax
import jax.numpy as jnp
from jax import lax
from jax.experimental import pallas as pl
from jax.experimental.pallas import tpu as pltpu
from jax.sharding import PartitionSpec as P

HEAD = 64


EPS = 1e-05
NEGATIVE = -1e30
VMEM_LIMIT = 24 * 1024 * 1024


def swap_cores(part):
    return lax.ppermute(part, "tensor", [(0, 1), (1, 0)])


STEP_X, STEP_Y, STEP_Z, STEP_W = 1, 2, 4, 12
ORDERS = (
    (STEP_X, STEP_Y, STEP_Z, STEP_W),
    (STEP_Y, STEP_X, STEP_Z, STEP_W),
    (STEP_Z, STEP_W, STEP_X, STEP_Y),
)


def relative_block(order, place):
    steps = len(order)
    block = 0
    for position, mask in enumerate(order):
        if (place >> (steps - 1 - position)) & 1:
            block ^= mask
    return block


def dot(left, right, contract=((1,), (0,))):
    return lax.dot_general(left, right, (contract, ((), ())), preferred_element_type=jnp.float32)


NT = ((1,), (1,))
TN = ((0,), (0,))


def run_kernel(body, name, outputs, operands, scalars=(), scratch=(), flops=0):
    moved = sum(array.size * array.dtype.itemsize for array in operands)
    moved += sum(math.prod(shape) * jnp.dtype(dtype).itemsize for shape, dtype in outputs)
    return pl.pallas_call(
        body,
        out_shape=tuple(jax.ShapeDtypeStruct(shape, dtype) for shape, dtype in outputs),
        in_specs=[pl.BlockSpec(memory_space=pltpu.SMEM)] * len(scalars)
        + [pl.BlockSpec(memory_space=pltpu.VMEM)] * len(operands),
        out_specs=tuple([pl.BlockSpec(memory_space=pltpu.VMEM)] * len(outputs)),
        scratch_shapes=list(scratch),
        compiler_params=pltpu.CompilerParams(vmem_limit_bytes=VMEM_LIMIT),
        cost_estimate=pl.CostEstimate(flops=flops, bytes_accessed=moved, transcendentals=0),
        name=name,
    )(*scalars, *operands)


def square_iota(size):
    return lax.broadcasted_iota(jnp.int32, (size, size), 0), lax.broadcasted_iota(jnp.int32, (size, size), 1)


def halves(values):
    high = values.astype(jnp.bfloat16)
    return high, (values - high.astype(jnp.float32)).astype(jnp.bfloat16)


def same_span(spans_ref, row):
    span_row = spans_ref[row : row + 1, :].astype(jnp.float32)
    down, along = square_iota(span_row.shape[1])
    eye = down == along
    span_col = jnp.sum(jnp.where(eye, span_row, 0.0), 1, keepdims=True)
    return span_col == span_row, eye


def head_masks():
    lane = lax.broadcasted_iota(jnp.int32, (1, 2 * HEAD), 1)
    first = (lane < HEAD).astype(jnp.float32).astype(jnp.bfloat16)
    second = (lane >= HEAD).astype(jnp.float32).astype(jnp.bfloat16)
    return first, second


def pair_lanes(pair, start):
    return pl.ds(pl.multiple_of(start + pair * 2 * HEAD, 2 * HEAD), 2 * HEAD)


def norm_rows(resid):
    centered = resid - jnp.mean(resid, -1, keepdims=True)
    inv_std = lax.rsqrt(jnp.mean(centered * centered, -1, keepdims=True) + EPS)
    return centered * inv_std, inv_std


def norm_back(grad_in, gain_vec, normed, inv_std):
    d_normed = grad_in * gain_vec
    return inv_std * (
        d_normed
        - jnp.mean(d_normed, -1, keepdims=True)
        - normed * jnp.mean(d_normed * normed, -1, keepdims=True)
    )


def front_kernel(row, lengths_ref, hidden_ref, spans_ref, query_ref, w_qkv_ref, bias_ref, w_out_ref, *outs):
    pooled_ref, low_ref, qkv_ref, stats_ref, logs_ref, context_ref, part_ref = outs
    hidden = hidden_ref[row]
    seq, width = hidden.shape
    local = context_ref.shape[1]
    heads = local // HEAD
    inputs = hidden.astype(jnp.float32)
    score = jnp.sum(inputs * query_ref[...], 1, keepdims=True)
    same, eye = same_span(spans_ref, row)
    score_row = jnp.sum(jnp.where(eye, score, 0.0), 0, keepdims=True)
    top_row = jnp.max(jnp.where(same, score, NEGATIVE), 0, keepdims=True)
    weight_row = jnp.exp(score_row - top_row)
    weight = jnp.sum(jnp.where(eye, weight_row, 0.0), 1, keepdims=True)
    spread = jnp.where(same, weight_row, 0.0)
    total = jnp.sum(spread, 1, keepdims=True)
    high, low = halves(spread)
    pooled = (dot(high, hidden) + dot(low, hidden)) / total
    pooled_ref[...] = pooled
    low_ref[...] = (inputs + pooled).astype(jnp.bfloat16)
    lane = lax.broadcasted_iota(jnp.int32, (1, 128), 1)
    stats_ref[...] = jnp.where(lane == heads, total, jnp.where(lane == heads + 1, weight, 0.0))
    for part in range(3):
        columns = slice(part * local, (part + 1) * local)
        proj = dot(low_ref[...], w_qkv_ref[:, columns]) + bias_ref[:, columns]
        if part == 0:
            proj = proj * (1.0 / math.sqrt(HEAD))
        qkv_ref[:, columns] = proj.astype(jnp.bfloat16)
    valid = lax.broadcasted_iota(jnp.int32, (1, seq), 1) < lengths_ref[row]
    masks = head_masks()
    block = seq // 2

    def attend(pair, carry):
        query = qkv_ref[:, pair_lanes(pair, 0)]
        key = qkv_ref[:, pair_lanes(pair, local)]
        value = qkv_ref[:, pair_lanes(pair, 2 * local)]
        for step in range(2):
            rows = slice(step * block, (step + 1) * block)
            context = None
            stats = stats_ref[rows, :]
            for half in range(2):
                scores = dot(query[rows] * masks[half], key, NT)
                scores = jnp.where(valid, scores, NEGATIVE)
                top = jnp.max(scores, -1, keepdims=True)
                expo = jnp.exp(scores - top)
                expo_sum = jnp.sum(expo, -1, keepdims=True)
                probs = (expo * (1.0 / expo_sum)).astype(jnp.bfloat16)
                piece = dot(probs, value * masks[half])
                context = piece if context is None else context + piece
                stats = jnp.where(lane == 2 * pair + half, top + jnp.log(expo_sum), stats)
            stats_ref[rows, :] = stats
            context_ref[rows, pair_lanes(pair, 0)] = context.astype(jnp.bfloat16)
        return carry

    lax.fori_loop(0, heads // 2, attend, 0)
    logs_ref[...] = jnp.transpose(stats_ref[...])[: logs_ref.shape[0]]
    part_ref[...] = dot(context_ref[...], w_out_ref[...], NT)


def mid_kernel(row, hidden_ref, pooled_ref, part_ref, other_ref, biases_ref, gains_ref, shifts_ref, w_up_ref, up_bias_ref, w_down_ref, *outs):
    normed_ref, inv_ref, low_ref, act_ref, slope_ref, down_ref = outs
    resid = hidden_ref[row].astype(jnp.float32) + pooled_ref[...]
    resid = resid + ((part_ref[...] + other_ref[...]) + biases_ref[0:1, :])
    normed, inv_std = norm_rows(resid)
    normed_ref[...] = normed
    inv_ref[...] = inv_std
    low_ref[...] = (normed * gains_ref[0:1, :] + shifts_ref[0:1, :]).astype(jnp.bfloat16)
    chunk, step = 256, 64
    total = None
    for start in range(0, act_ref.shape[1], chunk):
        columns = slice(start, start + chunk)
        up = dot(low_ref[...], w_up_ref[:, columns]) + up_bias_ref[:, columns]
        for first in range(0, up.shape[0], step):
            rows = slice(first, first + step)
            piece = up[rows]
            cdf = 0.5 * (1.0 + lax.erf(piece * math.sqrt(0.5)))
            density = jnp.exp(piece * piece * -0.5) * (1.0 / math.sqrt(2.0 * math.pi))
            act_ref[rows, columns] = (piece * cdf).astype(jnp.bfloat16)
            slope_ref[rows, columns] = cdf + piece * density
        down = dot(act_ref[:, columns], w_down_ref[:, columns], NT)
        total = down if total is None else total + down
    down_ref[...] = total


def turn_kernel(row, lengths_ref, normed_ref, down_ref, other_ref, cotangent_ref, biases_ref, gains_ref, shifts_ref, *outs):
    out_ref, d_down_ref, d_down_low_ref, sums_ref = outs
    seq = normed_ref.shape[0]
    first_norm = normed_ref[...] * gains_ref[0:1, :] + shifts_ref[0:1, :]
    normed, inv_std = norm_rows(first_norm + ((down_ref[...] + other_ref[...]) + biases_ref[1:2, :]))
    out_ref[...] = (normed * gains_ref[1:2, :] + shifts_ref[1:2, :]).astype(jnp.bfloat16)
    valid = (lax.broadcasted_iota(jnp.int32, (seq, 1), 0) < lengths_ref[row]).astype(jnp.float32)
    d_out = cotangent_ref[row].astype(jnp.float32) * valid
    sums_ref[0:1, :] = jnp.sum(d_out * normed, 0, keepdims=True)
    sums_ref[1:2, :] = jnp.sum(d_out, 0, keepdims=True)
    d_down = norm_back(d_out, gains_ref[1:2, :], normed, inv_std)
    sums_ref[2:3, :] = jnp.sum(d_down, 0, keepdims=True)
    sums_ref[3:8, :] = jnp.zeros((5, sums_ref.shape[1]), jnp.float32)
    d_down_ref[...] = d_down
    d_down_low_ref[...] = d_down.astype(jnp.bfloat16)


def units_kernel(lengths_ref, d_down_low_ref, slope_ref, w_up_ref, w_down_ref, *outs):
    d_up_ref, back_ref, up_sums_ref = outs
    chunk = 256
    total = None
    for start in range(0, d_up_ref.shape[1], chunk):
        columns = slice(start, start + chunk)
        d_up = dot(d_down_low_ref[...], w_down_ref[:, columns]) * slope_ref[:, columns]
        up_sums_ref[:, columns] = jnp.sum(d_up, 0, keepdims=True)
        d_up_ref[:, columns] = d_up.astype(jnp.bfloat16)
        back = dot(d_up_ref[:, columns], w_up_ref[:, columns], NT)
        total = back if total is None else total + back
    back_ref[...] = total


def back_kernel(row, lengths_ref, back_ref, other_ref, d_down_ref, normed_ref, inv_ref, gains_ref, qkv_ref, logs_ref, w_out_ref, w_qkv_ref, *outs):
    d_attn_ref, d_attn_low_ref, d_proj_ref, join_ref, sums_ref, qv_sums_ref, d_context_ref = outs
    seq = back_ref.shape[0]
    local = d_context_ref.shape[1]
    normed = normed_ref[...]
    d_first = (back_ref[...] + other_ref[...]) + d_down_ref[...]
    sums_ref[0:1, :] = jnp.sum(d_first * normed, 0, keepdims=True)
    sums_ref[1:2, :] = jnp.sum(d_first, 0, keepdims=True)
    d_attn = norm_back(d_first, gains_ref[0:1, :], normed, inv_ref[...])
    sums_ref[2:3, :] = jnp.sum(d_attn, 0, keepdims=True)
    sums_ref[3:8, :] = jnp.zeros((5, sums_ref.shape[1]), jnp.float32)
    d_attn_ref[...] = d_attn
    d_attn_low_ref[...] = d_attn.astype(jnp.bfloat16)
    d_context_ref[...] = dot(d_attn_low_ref[...], w_out_ref[...]).astype(jnp.bfloat16)
    scale = 1.0 / math.sqrt(HEAD)
    masks = head_masks()
    block = seq // 2
    valid = lax.broadcasted_iota(jnp.int32, (seq, 1), 0) < lengths_ref[row]

    def attend(pair, carry):
        query = qkv_ref[:, pair_lanes(pair, 0)]
        key = qkv_ref[:, pair_lanes(pair, local)]
        value = qkv_ref[:, pair_lanes(pair, 2 * local)]
        grad = d_context_ref[:, pair_lanes(pair, 0)]
        d_key = d_value = None
        query_sum = jnp.zeros((1, 2 * HEAD), jnp.float32)
        for step in range(2):
            columns = slice(step * block, (step + 1) * block)
            d_query = None
            for half in range(2):
                query_part = query[columns] * masks[half]
                grad_part = grad[columns] * masks[half]
                scores = jnp.where(valid, dot(key, query_part, NT), NEGATIVE)
                probs = jnp.exp(scores - logs_ref[pl.ds(2 * pair + half, 1), columns])
                d_probs = dot(value, grad_part, NT)
                piece = dot(probs.astype(jnp.bfloat16), grad_part)
                d_value = piece if d_value is None else d_value + piece
                d_scores = probs * (d_probs - jnp.sum(d_probs * probs, 0, keepdims=True))
                d_scores = d_scores.astype(jnp.bfloat16)
                piece = dot(d_scores, query_part)
                d_key = piece if d_key is None else d_key + piece
                piece = dot(d_scores, key * masks[half], TN)
                d_query = piece if d_query is None else d_query + piece
            d_query = d_query * scale
            query_sum = query_sum + jnp.sum(d_query, 0, keepdims=True)
            d_proj_ref[columns, pair_lanes(pair, 0)] = d_query.astype(jnp.bfloat16)
        d_proj_ref[:, pair_lanes(pair, local)] = d_key.astype(jnp.bfloat16)
        d_proj_ref[:, pair_lanes(pair, 2 * local)] = d_value.astype(jnp.bfloat16)
        qv_sums_ref[0:1, pair_lanes(pair, 0)] = query_sum
        qv_sums_ref[1:2, pair_lanes(pair, 0)] = jnp.sum(d_value, 0, keepdims=True)
        return carry

    lax.fori_loop(0, local // (2 * HEAD), attend, 0)
    join_ref[...] = dot(d_proj_ref[...], w_qkv_ref[...], NT)


def join_back_kernel(rows, heads, lengths_ref, hidden_ref, spans_ref, query_ref, *refs):
    grad_ref, sums_ref = refs[-2:]
    query = query_ref[...]
    for row in range(rows):
        join_ref, other_ref, d_attn_ref, pooled_ref, stats_ref = refs[5 * row : 5 * row + 5]
        hidden = hidden_ref[row]
        inputs = hidden.astype(jnp.float32)
        total = stats_ref[:, heads : heads + 1]
        weight = stats_ref[:, heads + 1 : heads + 2]
        d_joined = (join_ref[...] + other_ref[...]) + d_attn_ref[...]
        d_total = -jnp.sum(d_joined * pooled_ref[...], 1, keepdims=True) / total
        same, eye = same_span(spans_ref, row)
        d_total_row = jnp.sum(jnp.where(eye, d_total, 0.0), 0, keepdims=True)
        high, low = halves(d_joined / total)
        chosen = same.astype(jnp.float32).astype(jnp.bfloat16)
        d_weighted = dot(chosen, high) + dot(chosen, low)
        d_weight = jnp.sum(jnp.where(same, d_total_row, 0.0), 1, keepdims=True)
        d_weight = d_weight + jnp.sum(d_weighted * inputs, 1, keepdims=True)
        d_score = weight * d_weight
        grad_ref[row] = d_joined + weight * d_weighted + d_score * query
        sums = jnp.sum(d_score * inputs, 0, keepdims=True)
        if row == 0:
            sums_ref[...] = sums
        else:
            sums_ref[...] = sums_ref[...] + sums


def grad_kernel(parts, rows, *refs):
    here_ref = refs[0]
    count = sum(2 * terms for _, terms in parts)
    operands = refs[1 : 1 + count]
    outs = refs[1 + count : 7 + count]
    turned = refs[7 + count : 7 + count + len(parts)]
    totals = refs[7 + count + len(parts) : -1]
    sem = refs[-1]
    here = here_ref[0]
    copies = []
    first = 0
    for part, (_, terms) in enumerate(parts):
        for term in range(terms):
            left = operands[first + 2 * term]
            size = left.shape[0]
            turned[part][:, term * size : (term + 1) * size] = jnp.transpose(left[...])
        first += 2 * terms
    slot = 0
    for colour, order in enumerate(ORDERS):
        column = first = 0
        for part, (ranges, terms) in enumerate(parts):
            start, width = ranges[colour]
            if width:
                total = totals[slot]
                slot += 1
                product = None
                for term in range(terms):
                    right = operands[first + 2 * term + 1]
                    size = right.shape[0]
                    left = turned[part][:, term * size : (term + 1) * size]
                    piece = dot(left, right[:, start : start + width])
                    product = piece if product is None else product + piece
                total[...] = product
                for place in range(16):
                    block = jnp.bitwise_xor(here, relative_block(order, place))
                    source = total.at[pl.ds(pl.multiple_of(block * rows, 8), rows), :]
                    target = outs[2 * colour + place // 8].at[place % 8, :, pl.ds(column, width)]
                    copy = pltpu.make_async_copy(source, target, sem.at[colour])
                    copy.start()
                    copies.append(copy)
                column += width
            first += 2 * terms
    for copy in copies:
        copy.wait()


def grad_blocks(here, operands, parts):
    height = operands[0][0][0].shape[1]
    rows = height // 16
    widths = [sum(ranges[colour][1] for ranges in parts) for colour in range(3)]
    out_shape = []
    for width in widths:
        out_shape += [jax.ShapeDtypeStruct((8, rows, width), jnp.float32)] * 2
    scratch = [pltpu.VMEM((height, sum(left.shape[0] for left, _ in pairs)), jnp.bfloat16) for pairs in operands]
    for colour in range(3):
        for ranges in parts:
            if ranges[colour][1]:
                scratch.append(pltpu.VMEM((height, ranges[colour][1]), jnp.float32))
    flat = [array for pairs in operands for pair in pairs for array in pair]
    flops = sum(2 * left.size * right.shape[1] for pairs in operands for left, right in pairs)
    moved = sum(2 * array.size for array in flat) + sum(4 * 16 * rows * width for width in widths)
    return pl.pallas_call(
        functools.partial(grad_kernel, [(ranges, len(pairs)) for ranges, pairs in zip(parts, operands)], rows),
        out_shape=tuple(out_shape),
        in_specs=[pl.BlockSpec(memory_space=pltpu.SMEM)] + [pl.BlockSpec(memory_space=pltpu.VMEM)] * len(flat),
        out_specs=tuple([pl.BlockSpec(memory_space=pl.ANY)] * 6),
        scratch_shapes=scratch + [pltpu.SemaphoreType.DMA((3,))],
        compiler_params=pltpu.CompilerParams(vmem_limit_bytes=VMEM_LIMIT),
        cost_estimate=pl.CostEstimate(flops=flops, bytes_accessed=moved, transcendentals=0),
        name="weight_grads",
    )(here, *flat)


def scatter_start(blocks, token):
    keeps = [blocks[2 * colour] for colour in range(3)]
    sends = [blocks[2 * colour + 1] for colour in range(3)]
    state = {"keeps": keeps, "arrived": [[] for _ in ORDERS], "half": 8, "step": 0}
    return state, scatter_send(state, sends, token)


def scatter_send(state, sends, token):
    sends, token = lax.optimization_barrier((sends, token))
    state["incoming"] = [
        lax.ppermute(sends[colour], "dp", [(i, i ^ order[state["step"]]) for i in range(16)])
        for colour, order in enumerate(ORDERS)
    ]
    state["step"] += 1
    return token


def scatter_next(state, token, *done):
    incoming, token, _ = lax.optimization_barrier((state["incoming"], token, done))
    state["half"] //= 2
    half = state["half"]
    sends = []
    for colour in range(3):
        state["arrived"][colour].append(incoming[colour])
        if half:
            total = state["keeps"][colour][half : 2 * half]
            for array in state["arrived"][colour]:
                total = total + array[half : 2 * half]
            sends.append(total)
    return scatter_send(state, sends, token) if half else token


def scatter_result(state):
    results = []
    for colour in range(3):
        total = state["keeps"][colour][0]
        for array in state["arrived"][colour]:
            total = total + array[0]
        results.append(total)
    return results


def all_sum(values):
    for mask in (STEP_X, STEP_Y, STEP_Z, STEP_W):
        values = values + lax.ppermute(values, "dp", [(i, i ^ mask) for i in range(16)])
    return values


def per_device(
    spread,
    hidden,
    lengths,
    spans,
    join_query,
    w_qkv,
    qv_bias,
    w_out,
    out_biases,
    norm_gains,
    norm_biases,
    w_up,
    up_bias,
    w_down,
    cotangent,
):
    row_count, seq, width = hidden.shape
    local = w_qkv.shape[2]
    units = w_up.shape[1]
    heads = local // HEAD
    rows = range(row_count)
    f32, bf16 = jnp.float32, jnp.bfloat16
    query_row = join_query.reshape(1, width)
    w_qkv_flat = w_qkv.reshape(width, 3 * local)
    qkv_bias = jnp.concatenate([qv_bias[0], jnp.zeros((local,), f32), qv_bias[1]]).reshape(1, 3 * local)
    up_bias_row = up_bias.reshape(1, units)
    log_rows = 8 * (-(-heads // 8))

    front = []
    for row in rows:
        front.append(
            run_kernel(
                functools.partial(front_kernel, row),
                "front",
                (
                    ((seq, width), f32),
                    ((seq, width), bf16),
                    ((seq, 3 * local), bf16),
                    ((seq, 128), f32),
                    ((log_rows, seq), f32),
                    ((seq, local), bf16),
                    ((seq, width), f32),
                ),
                (hidden, spans, query_row, w_qkv_flat, qkv_bias, w_out),
                (lengths,),
                flops=2 * seq * (2 * seq * width + 4 * width * local + 2 * seq * local),
            )
        )
    pooled, joined_low, qkv, stats, logs, context_low, attn_part = zip(*front)
    mid = []
    for row in rows:
        mid.append(
            run_kernel(
                functools.partial(mid_kernel, row),
                "mid",
                (
                    ((seq, width), f32),
                    ((seq, 1), f32),
                    ((seq, width), bf16),
                    ((seq, units), bf16),
                    ((seq, units), f32),
                    ((seq, width), f32),
                ),
                (
                    hidden,
                    pooled[row],
                    attn_part[row],
                    swap_cores(attn_part[row]),
                    out_biases,
                    norm_gains,
                    norm_biases,
                    w_up,
                    up_bias_row,
                    w_down,
                ),
                flops=4 * seq * width * units,
            )
        )
    normed, inv_std, first_low, act_low, slope, down_part = zip(*mid)
    turn = []
    for row in rows:
        turn.append(
            run_kernel(
                functools.partial(turn_kernel, row),
                "turn",
                (((seq, width), bf16), ((seq, width), f32), ((seq, width), bf16), ((8, width), f32)),
                (
                    normed[row],
                    down_part[row],
                    swap_cores(down_part[row]),
                    cotangent,
                    out_biases,
                    norm_gains,
                    norm_biases,
                ),
                (lengths,),
                flops=seq * width,
            )
        )
    layer_out, d_down, d_down_low, turn_sums = zip(*turn)
    scattered = spread == 16 and width % 128 == 0
    token = lengths
    if scattered:
        here = lax.axis_index("dp").astype(jnp.int32).reshape(1)
        unit = units // 12
        down_cols = ((0, 5 * unit), (5 * unit, 4 * unit), (9 * unit, 3 * unit))
        up_cols = ((0, 4 * unit), (4 * unit, 5 * unit), (9 * unit, 3 * unit))
        out_cols = ((0, 0), (0, 0), (0, local))
        qkv_cols = ((0, 5 * local // 3), (5 * local // 3, 4 * local // 3), (0, 0))
        down_blocks = grad_blocks(here, [list(zip(d_down_low, act_low))], [down_cols])
        down_sum, token = scatter_start(down_blocks, token)
    ffn_back = []
    for row in rows:
        ffn_back.append(
            run_kernel(
                units_kernel,
                "units",
                (((seq, units), bf16), ((seq, width), f32), ((1, units), f32)),
                (d_down_low[row], slope[row], w_up, w_down),
                (token,),
                flops=4 * seq * width * units,
            )
        )
    d_up_low, back_part, up_sums = zip(*ffn_back)
    if scattered:
        token = scatter_next(down_sum, token, up_sums)
        here, token = lax.optimization_barrier((here, token))
        up_blocks = grad_blocks(here, [list(zip(first_low, d_up_low))], [up_cols])
        up_sum, token = scatter_start(up_blocks, token)
    back = []
    for row in rows:
        back.append(
            run_kernel(
                functools.partial(back_kernel, row),
                "back",
                (
                    ((seq, width), f32),
                    ((seq, width), bf16),
                    ((seq, 3 * local), bf16),
                    ((seq, width), f32),
                    ((8, width), f32),
                    ((2, local), f32),
                    ((seq, local), bf16),
                ),
                (
                    back_part[row],
                    swap_cores(back_part[row]),
                    d_down[row],
                    normed[row],
                    inv_std[row],
                    norm_gains,
                    qkv[row],
                    logs[row],
                    w_out,
                    w_qkv_flat,
                ),
                (token,),
                flops=2 * seq * (4 * width * local + 5 * seq * local),
            )
        )
        if scattered:
            token = scatter_next(down_sum, token, back[-1][4])
            if row == row_count - 1:
                token = scatter_next(up_sum, token, back[-1][4])
    d_attn, d_attn_low, d_proj, join_part, back_sums, qv_sums, _ = zip(*back)
    if scattered:
        here, token = lax.optimization_barrier((here, token))
        rest_blocks = grad_blocks(
            here, [list(zip(d_attn_low, context_low)), list(zip(joined_low, d_proj))], [out_cols, qkv_cols]
        )
        rest_sum, token = scatter_start(rest_blocks, token)
        token = scatter_next(up_sum, token)
    joined_back = []
    for row in rows:
        joined_back += [join_part[row], swap_cores(join_part[row]), d_attn[row], pooled[row], stats[row]]
    grad_inputs, join_grad = run_kernel(
        functools.partial(join_back_kernel, row_count, heads),
        "join_back",
        (((row_count, seq, width), f32), ((1, width), f32)),
        (hidden, spans, query_row, *joined_back),
        (token,),
        flops=4 * row_count * seq * seq * width,
    )
    turn_sum = sum(turn_sums[1:], turn_sums[0])
    back_sum = sum(back_sums[1:], back_sums[0])
    small = (
        sum(qv_sums[1:], qv_sums[0]),
        sum(up_sums[1:], up_sums[0]).reshape(units),
        jnp.stack([back_sum[2], turn_sum[2]]),
        jnp.stack([back_sum[0], turn_sum[0]]),
        jnp.stack([back_sum[1], turn_sum[1]]),
        join_grad.reshape(width),
    )
    if scattered:
        token = scatter_next(down_sum, token, join_grad)
        token = scatter_next(up_sum, token, join_grad)
        for _ in range(4):
            token = scatter_next(rest_sum, token, join_grad)
        token = scatter_next(up_sum, token, join_grad)
        down_rows = jnp.concatenate(scatter_result(down_sum), axis=1)
        up_rows = jnp.concatenate(scatter_result(up_sum), axis=1)
        rest = scatter_result(rest_sum)
        out_rows = rest[2]
        qkv_rows = jnp.concatenate(rest[:2], axis=1).reshape(-1, 3, local)
        sizes = [math.prod(value.shape) for value in small]
        packed = all_sum(jnp.concatenate([value.reshape(-1) for value in small]).reshape(-1, 128)).reshape(-1)
        summed, offset = [], 0
        for value, size in zip(small, sizes):
            summed.append(packed[offset : offset + size].reshape(value.shape))
            offset += size
    else:

        def first_product(lefts, rights):
            total = sum(dot(left, right, TN) for left, right in zip(lefts, rights))
            return lax.psum_scatter(total, "dp", scatter_dimension=0, tiled=True)

        down_rows = first_product(d_down_low, act_low)
        up_rows = first_product(first_low, d_up_low)
        out_rows = first_product(d_attn_low, context_low)
        qkv_rows = first_product(joined_low, d_proj).reshape(-1, 3, local)
        summed = lax.psum(small, "dp")
    return (
        jnp.stack(layer_out),
        grad_inputs,
        qkv_rows,
        summed[0],
        out_rows,
        summed[2],
        summed[3],
        summed[4],
        up_rows,
        summed[1],
        down_rows,
        summed[5],
    )


def solution(mesh):
    return jax.shard_map(
        functools.partial(per_device, mesh.shape["dp"]),
        mesh=mesh,
        in_specs=(
            P("dp", None, None),
            P("dp"),
            P("dp", None),
            P(),
            P(None, None, "tensor"),
            P(None, "tensor"),
            P(None, "tensor"),
            P(),
            P(),
            P(),
            P(None, "tensor"),
            P("tensor"),
            P(None, "tensor"),
            P("dp", None, None),
        ),
        out_specs=(
            P("dp", None, None),
            P("dp", None, None),
            P("dp", None, "tensor"),
            P(None, "tensor"),
            P("dp", "tensor"),
            P(),
            P(),
            P(),
            P("dp", "tensor"),
            P("tensor"),
            P("dp", "tensor"),
            P(),
        ),
        check_vma=False,
    )
```

```python
import functools
import math

import jax
import jax.numpy as jnp
from jax import lax
from jax.experimental import pallas as pl
from jax.experimental.pallas import tpu as pltpu
from jax.sharding import PartitionSpec as P

HEAD = 64


EPS = 1e-05
NEGATIVE = -1e30
MEGA = 1024 * 1024
SMALL = 64 * 1024


def swap_cores(part):
    return lax.ppermute(part, "tensor", [(0, 1), (1, 0)])


STEP_X, STEP_Y, STEP_Z, STEP_W = 1, 2, 4, 12
ORDERS = (
    (STEP_X, STEP_Y, STEP_Z, STEP_W),
    (STEP_Y, STEP_X, STEP_Z, STEP_W),
    (STEP_Z, STEP_W, STEP_X, STEP_Y),
)


def relative_block(order, place):
    steps = len(order)
    block = 0
    for position, mask in enumerate(order):
        if (place >> (steps - 1 - position)) & 1:
            block ^= mask
    return block


def dot(left, right, contract=((1,), (0,))):
    return lax.dot_general(left, right, (contract, ((), ())), preferred_element_type=jnp.float32)


NT = ((1,), (1,))
TN = ((0,), (0,))


class Arriving:
    def __init__(self, source, place, sem):
        self.copy, self.place, self.shape, self.waited = pltpu.make_async_copy(source, place, sem), place, place.shape, False
        self.copy.start()

    def ready(self):
        if not self.waited:
            self.copy.wait()
            self.waited = True
        return self.place

    def __getitem__(self, index):
        return self.ready()[index]


class Leaving:
    def __init__(self, place, target, sem):
        self.place, self.target, self.sem, self.shape, self.copies = place, target, sem, place.shape, []

    def __getitem__(self, index):
        return self.place[index]

    def __setitem__(self, index, value):
        self.place[index] = value

    def send(self, rows=slice(None), columns=slice(None)):
        if len(self.shape) == 2:
            source, target = self.place.at[rows, columns], self.target.at[rows, columns]
        else:
            source, target = self.place, self.target
        self.copies.append(pltpu.make_async_copy(source, target, self.sem))
        self.copies[-1].start()

    def finish(self):
        if not self.copies:
            self.send()
        for copy in self.copies:
            copy.wait()


def moving_kernel(body, row, flags, scalar_count, *refs):
    count = len(flags)
    scalars, arrays, rest = refs[:scalar_count], refs[scalar_count : scalar_count + count], list(refs[scalar_count + count :])
    sems = rest.pop()
    views, leaving = [], []
    for index, (flag, array) in enumerate(zip(flags, arrays)):
        if flag == "small":
            views.append(array)
        elif flag == "out":
            views.append(Leaving(rest.pop(0), array, sems.at[index]))
            leaving.append(views[-1])
        else:
            source = array.at[row] if flag == "row" else array
            views.append(Arriving(source, rest.pop(0), sems.at[index]))
    body(*scalars, *views)
    for view in views:
        if isinstance(view, Arriving):
            view.ready()
    for view in leaving:
        view.finish()


def in_hbm(array):
    return pltpu.with_memory_space_constraint(array, pltpu.HBM)


def in_vmem(array):
    return pltpu.with_memory_space_constraint(array, pltpu.VMEM)


def run_kernel(body, name, outputs, operands, scalars=(), row=None, flops=0, room=12):
    flags, arrays, places, specs = [], [], [], []
    small_spec, large_spec = pl.BlockSpec(memory_space=pltpu.VMEM), pl.BlockSpec(memory_space=pltpu.HBM)
    for operand in operands:
        by_row, placed = isinstance(operand, tuple), isinstance(operand, list)
        array = operand[0] if by_row or placed else operand
        small = placed or array.size < SMALL
        arrays.append(in_vmem(array) if placed else array if small else in_hbm(array))
        flags.append("small" if small else "row" if by_row else "whole")
        specs.append(small_spec if small else large_spec)
        if not small:
            places.append(pltpu.VMEM(array.shape[1:] if by_row else array.shape, array.dtype))
    out_specs, out_shapes = [], []
    for shape, dtype in outputs:
        small = math.prod(shape) < SMALL
        flags.append("small" if small else "out")
        out_specs.append(small_spec if small else large_spec)
        out_shapes.append(jax.ShapeDtypeStruct(shape, dtype) if small else pltpu.HBM(shape, dtype))
        if not small:
            places.append(pltpu.VMEM(shape, dtype))
    held = sum(math.prod(place.shape) * jnp.dtype(place.dtype).itemsize for place in places)
    return pl.pallas_call(
        functools.partial(moving_kernel, body, row, flags, len(scalars)),
        out_shape=tuple(out_shapes),
        in_specs=[pl.BlockSpec(memory_space=pltpu.SMEM)] * len(scalars) + specs,
        out_specs=tuple(out_specs),
        scratch_shapes=places + [pltpu.SemaphoreType.DMA((len(flags),))],
        compiler_params=pltpu.CompilerParams(vmem_limit_bytes=held + room * MEGA),
        cost_estimate=pl.CostEstimate(flops=flops, bytes_accessed=held, transcendentals=0),
        name=name,
    )(*scalars, *arrays)


def square_iota(size):
    return lax.broadcasted_iota(jnp.int32, (size, size), 0), lax.broadcasted_iota(jnp.int32, (size, size), 1)


def halves(values):
    high = values.astype(jnp.bfloat16)
    return high, (values - high.astype(jnp.float32)).astype(jnp.bfloat16)


def same_span(spans_ref, row):
    span_row = spans_ref[row : row + 1, :].astype(jnp.float32)
    down, along = square_iota(span_row.shape[1])
    eye = down == along
    span_col = jnp.sum(jnp.where(eye, span_row, 0.0), 1, keepdims=True)
    return span_col == span_row, eye


def head_masks():
    lane = lax.broadcasted_iota(jnp.int32, (1, 2 * HEAD), 1)
    first = (lane < HEAD).astype(jnp.float32).astype(jnp.bfloat16)
    second = (lane >= HEAD).astype(jnp.float32).astype(jnp.bfloat16)
    return first, second


def pair_lanes(pair, start):
    return pl.ds(pl.multiple_of(start + pair * 2 * HEAD, 2 * HEAD), 2 * HEAD)


def norm_rows(resid):
    centered = resid - jnp.mean(resid, -1, keepdims=True)
    inv_std = lax.rsqrt(jnp.mean(centered * centered, -1, keepdims=True) + EPS)
    return centered * inv_std, inv_std


def norm_back(grad_in, gain_vec, normed, inv_std):
    d_normed = grad_in * gain_vec
    return inv_std * (
        d_normed
        - jnp.mean(d_normed, -1, keepdims=True)
        - normed * jnp.mean(d_normed * normed, -1, keepdims=True)
    )


def front_kernel(row, lengths_ref, hidden_ref, spans_ref, query_ref, w_qkv_ref, bias_ref, w_out_ref, *outs):
    pooled_ref, low_ref, qkv_ref, stats_ref, logs_ref, context_ref, part_ref = outs
    hidden = hidden_ref[row]
    seq, width = hidden.shape
    local = context_ref.shape[1]
    heads = local // HEAD
    inputs = hidden.astype(jnp.float32)
    score = jnp.sum(inputs * query_ref[...], 1, keepdims=True)
    same, eye = same_span(spans_ref, row)
    score_row = jnp.sum(jnp.where(eye, score, 0.0), 0, keepdims=True)
    top_row = jnp.max(jnp.where(same, score, NEGATIVE), 0, keepdims=True)
    weight_row = jnp.exp(score_row - top_row)
    weight = jnp.sum(jnp.where(eye, weight_row, 0.0), 1, keepdims=True)
    spread = jnp.where(same, weight_row, 0.0)
    total = jnp.sum(spread, 1, keepdims=True)
    high, low = halves(spread)
    pooled = (dot(high, hidden) + dot(low, hidden)) / total
    pooled_ref[...] = pooled
    pooled_ref.send()
    low_ref[...] = (inputs + pooled).astype(jnp.bfloat16)
    low_ref.send()
    lane = lax.broadcasted_iota(jnp.int32, (1, 128), 1)
    stats_ref[...] = jnp.where(lane == heads, total, jnp.where(lane == heads + 1, weight, 0.0))
    for part in range(3):
        columns = slice(part * local, (part + 1) * local)
        proj = dot(low_ref[...], w_qkv_ref[:, columns]) + bias_ref[:, columns]
        if part == 0:
            proj = proj * (1.0 / math.sqrt(HEAD))
        qkv_ref[:, columns] = proj.astype(jnp.bfloat16)
    qkv_ref.send()
    valid = lax.broadcasted_iota(jnp.int32, (1, seq), 1) < lengths_ref[row]
    masks = head_masks()
    block = seq // 2

    def attend(pair, carry):
        query = qkv_ref[:, pair_lanes(pair, 0)]
        key = qkv_ref[:, pair_lanes(pair, local)]
        value = qkv_ref[:, pair_lanes(pair, 2 * local)]
        for step in range(2):
            rows = slice(step * block, (step + 1) * block)
            context = None
            stats = stats_ref[rows, :]
            for half in range(2):
                scores = dot(query[rows] * masks[half], key, NT)
                scores = jnp.where(valid, scores, NEGATIVE)
                top = jnp.max(scores, -1, keepdims=True)
                expo = jnp.exp(scores - top)
                expo_sum = jnp.sum(expo, -1, keepdims=True)
                probs = (expo * (1.0 / expo_sum)).astype(jnp.bfloat16)
                piece = dot(probs, value * masks[half])
                context = piece if context is None else context + piece
                stats = jnp.where(lane == 2 * pair + half, top + jnp.log(expo_sum), stats)
            stats_ref[rows, :] = stats
            context_ref[rows, pair_lanes(pair, 0)] = context.astype(jnp.bfloat16)
        return carry

    lax.fori_loop(0, heads // 2, attend, 0)
    context_ref.send()
    logs_ref[...] = jnp.transpose(stats_ref[...])[: logs_ref.shape[0]]
    for rows in (slice(0, block), slice(block, seq)):
        part_ref[rows, :] = dot(context_ref[rows, :], w_out_ref[...], NT)
        part_ref.send(rows=rows)


def mid_kernel(hidden_ref, pooled_ref, part_ref, other_ref, biases_ref, gains_ref, shifts_ref, w_up_ref, up_bias_ref, w_down_ref, *outs):
    normed_ref, inv_ref, low_ref, act_ref, slope_ref, down_ref = outs
    resid = hidden_ref[...].astype(jnp.float32) + pooled_ref[...]
    resid = resid + ((part_ref[...] + other_ref[...]) + biases_ref[0:1, :])
    normed, inv_std = norm_rows(resid)
    normed_ref[...] = normed
    normed_ref.send()
    inv_ref[...] = inv_std
    low_ref[...] = (normed * gains_ref[0:1, :] + shifts_ref[0:1, :]).astype(jnp.bfloat16)
    low_ref.send()
    chunk, step = 256, 64
    total = None
    for start in range(0, act_ref.shape[1], chunk):
        columns = slice(start, start + chunk)
        up = dot(low_ref[...], w_up_ref[:, columns]) + up_bias_ref[:, columns]
        for first in range(0, up.shape[0], step):
            rows = slice(first, first + step)
            piece = up[rows]
            cdf = 0.5 * (1.0 + lax.erf(piece * math.sqrt(0.5)))
            density = jnp.exp(piece * piece * -0.5) * (1.0 / math.sqrt(2.0 * math.pi))
            act_ref[rows, columns] = (piece * cdf).astype(jnp.bfloat16)
            slope_ref[rows, columns] = (cdf + piece * density).astype(jnp.bfloat16)
        down = dot(act_ref[:, columns], w_down_ref[:, columns], NT)
        total = down if total is None else total + down
        if start % (2 * chunk):
            act_ref.send(columns=slice(start - chunk, start + chunk))
            slope_ref.send(columns=slice(start - chunk, start + chunk))
    down_ref[...] = total


def turn_kernel(row, lengths_ref, normed_ref, down_ref, other_ref, cotangent_ref, biases_ref, gains_ref, shifts_ref, *outs):
    out_ref, d_down_ref, d_down_low_ref, sums_ref = outs
    seq = normed_ref.shape[0]
    first_norm = normed_ref[...] * gains_ref[0:1, :] + shifts_ref[0:1, :]
    normed, inv_std = norm_rows(first_norm + ((down_ref[...] + other_ref[...]) + biases_ref[1:2, :]))
    out_ref[...] = (normed * gains_ref[1:2, :] + shifts_ref[1:2, :]).astype(jnp.bfloat16)
    valid = (lax.broadcasted_iota(jnp.int32, (seq, 1), 0) < lengths_ref[row]).astype(jnp.float32)
    out_ref.send()
    d_out = cotangent_ref[...].astype(jnp.float32) * valid
    sums_ref[0:1, :] = jnp.sum(d_out * normed, 0, keepdims=True)
    sums_ref[1:2, :] = jnp.sum(d_out, 0, keepdims=True)
    d_down = norm_back(d_out, gains_ref[1:2, :], normed, inv_std)
    sums_ref[2:3, :] = jnp.sum(d_down, 0, keepdims=True)
    sums_ref[3:8, :] = jnp.zeros((5, sums_ref.shape[1]), jnp.float32)
    d_down_ref[...] = d_down
    d_down_low_ref[...] = d_down.astype(jnp.bfloat16)


def units_kernel(rows, token_ref, w_down_ref, w_up_ref, *refs):
    for row in range(rows):
        d_down_low_ref, slope_ref = refs[2 * row : 2 * row + 2]
        d_up_ref, back_ref, up_sums_ref = refs[2 * rows + 3 * row : 2 * rows + 3 + 3 * row]
        chunk = 256
        total = None
        for start in range(0, d_up_ref.shape[1], chunk):
            columns = slice(start, start + chunk)
            d_up = dot(d_down_low_ref[...], w_down_ref[:, columns]) * slope_ref[:, columns].astype(jnp.float32)
            up_sums_ref[:, columns] = jnp.sum(d_up, 0, keepdims=True)
            d_up_ref[:, columns] = d_up.astype(jnp.bfloat16)
            back = dot(d_up_ref[:, columns], w_up_ref[:, columns], NT)
            total = back if total is None else total + back
            if start % (2 * chunk):
                d_up_ref.send(columns=slice(start - chunk, start + chunk))
        back_ref[...] = total
        back_ref.send()


def back_kernel(row, lengths_ref, back_ref, other_ref, d_down_ref, normed_ref, inv_ref, gains_ref, qkv_ref, logs_ref, w_out_ref, w_qkv_ref, *outs):
    d_attn_ref, d_attn_low_ref, d_proj_ref, join_ref, sums_ref, qv_sums_ref, d_context_ref = outs
    seq = back_ref.shape[0]
    local = d_context_ref.shape[1]
    normed = normed_ref[...]
    d_first = (back_ref[...] + other_ref[...]) + d_down_ref[...]
    sums_ref[0:1, :] = jnp.sum(d_first * normed, 0, keepdims=True)
    sums_ref[1:2, :] = jnp.sum(d_first, 0, keepdims=True)
    d_attn = norm_back(d_first, gains_ref[0:1, :], normed, inv_ref[...])
    sums_ref[2:3, :] = jnp.sum(d_attn, 0, keepdims=True)
    sums_ref[3:8, :] = jnp.zeros((5, sums_ref.shape[1]), jnp.float32)
    d_attn_ref[...] = d_attn
    d_attn_ref.send()
    d_attn_low_ref[...] = d_attn.astype(jnp.bfloat16)
    d_attn_low_ref.send()
    d_context_ref[...] = dot(d_attn_low_ref[...], w_out_ref[...]).astype(jnp.bfloat16)
    qkv_ref.ready()
    scale = 1.0 / math.sqrt(HEAD)
    masks = head_masks()
    block = seq // 2
    valid = lax.broadcasted_iota(jnp.int32, (seq, 1), 0) < lengths_ref[row]

    def attend(pair, carry):
        query = qkv_ref[:, pair_lanes(pair, 0)]
        key = qkv_ref[:, pair_lanes(pair, local)]
        value = qkv_ref[:, pair_lanes(pair, 2 * local)]
        grad = d_context_ref[:, pair_lanes(pair, 0)]
        d_key = d_value = None
        query_sum = jnp.zeros((1, 2 * HEAD), jnp.float32)
        for step in range(2):
            columns = slice(step * block, (step + 1) * block)
            d_query = None
            for half in range(2):
                query_part = query[columns] * masks[half]
                grad_part = grad[columns] * masks[half]
                scores = jnp.where(valid, dot(key, query_part, NT), NEGATIVE)
                probs = jnp.exp(scores - logs_ref[pl.ds(2 * pair + half, 1), columns])
                d_probs = dot(value, grad_part, NT)
                piece = dot(probs.astype(jnp.bfloat16), grad_part)
                d_value = piece if d_value is None else d_value + piece
                d_scores = probs * (d_probs - jnp.sum(d_probs * probs, 0, keepdims=True))
                d_scores = d_scores.astype(jnp.bfloat16)
                piece = dot(d_scores, query_part)
                d_key = piece if d_key is None else d_key + piece
                piece = dot(d_scores, key * masks[half], TN)
                d_query = piece if d_query is None else d_query + piece
            d_query = d_query * scale
            query_sum = query_sum + jnp.sum(d_query, 0, keepdims=True)
            d_proj_ref[columns, pair_lanes(pair, 0)] = d_query.astype(jnp.bfloat16)
        d_proj_ref[:, pair_lanes(pair, local)] = d_key.astype(jnp.bfloat16)
        d_proj_ref[:, pair_lanes(pair, 2 * local)] = d_value.astype(jnp.bfloat16)
        qv_sums_ref[0:1, pair_lanes(pair, 0)] = query_sum
        qv_sums_ref[1:2, pair_lanes(pair, 0)] = jnp.sum(d_value, 0, keepdims=True)
        return carry

    lax.fori_loop(0, local // (2 * HEAD), attend, 0)
    d_proj_ref.send()
    join_ref[...] = dot(d_proj_ref[...], w_qkv_ref[...], NT)


def join_back_kernel(row, heads, lengths_ref, hidden_ref, spans_ref, query_ref, join_ref, other_ref, d_attn_ref, pooled_ref, stats_ref, *outs):
    grad_ref, sums_ref = outs
    total = stats_ref[:, heads : heads + 1]
    weight = stats_ref[:, heads + 1 : heads + 2]
    d_joined = (join_ref[...] + other_ref[...]) + d_attn_ref[...]
    d_total = -jnp.sum(d_joined * pooled_ref[...], 1, keepdims=True) / total
    same, eye = same_span(spans_ref, row)
    d_total_row = jnp.sum(jnp.where(eye, d_total, 0.0), 0, keepdims=True)
    high, low = halves(d_joined / total)
    chosen = same.astype(jnp.float32).astype(jnp.bfloat16)
    d_weighted = dot(chosen, high) + dot(chosen, low)
    inputs = hidden_ref[...].astype(jnp.float32)
    d_weight = jnp.sum(jnp.where(same, d_total_row, 0.0), 1, keepdims=True)
    d_weight = d_weight + jnp.sum(d_weighted * inputs, 1, keepdims=True)
    d_score = weight * d_weight
    grad_ref[...] = d_joined + weight * d_weighted + d_score * query_ref[...]
    grad_ref.send()
    sums_ref[...] = jnp.sum(d_score * inputs, 0, keepdims=True)


def grad_kernel(parts, rows, *refs):
    here_ref = refs[0]
    count = sum(2 * terms for _, terms in parts)
    sources = refs[1 : 1 + count]
    outs = refs[1 + count : 7 + count]
    places = refs[7 + count : 7 + 2 * count]
    turned = refs[7 + 2 * count : 7 + 2 * count + len(parts)]
    totals = refs[7 + 2 * count + len(parts) : -2]
    in_sems, sem = refs[-2:]
    here = here_ref[0]
    order_in = list(range(0, count, 2)) + list(range(1, count, 2))
    operands = {index: Arriving(sources[index], places[index], in_sems.at[index]) for index in order_in}
    copies = []
    first = 0
    for part, (_, terms) in enumerate(parts):
        for term in range(terms):
            left = operands[first + 2 * term]
            size = left.shape[0]
            turned[part][:, term * size : (term + 1) * size] = jnp.transpose(left[...])
        first += 2 * terms
    slot = 0
    for colour, order in enumerate(ORDERS):
        column = first = 0
        for part, (ranges, terms) in enumerate(parts):
            start, width = ranges[colour]
            if width:
                total = totals[slot]
                slot += 1
                product = None
                for term in range(terms):
                    right = operands[first + 2 * term + 1]
                    size = right.shape[0]
                    left = turned[part][:, term * size : (term + 1) * size]
                    piece = dot(left, right[:, start : start + width])
                    product = piece if product is None else product + piece
                total[...] = product
                for place in range(16):
                    block = jnp.bitwise_xor(here, relative_block(order, place))
                    source = total.at[pl.ds(pl.multiple_of(block * rows, 8), rows), :]
                    target = outs[2 * colour + place // 8].at[place % 8, :, pl.ds(column, width)]
                    copy = pltpu.make_async_copy(source, target, sem.at[colour])
                    copy.start()
                    copies.append(copy)
                column += width
            first += 2 * terms
    for copy in copies:
        copy.wait()


def grad_blocks(here, operands, parts):
    height = operands[0][0][0].shape[1]
    rows = height // 16
    widths = [sum(ranges[colour][1] for ranges in parts) for colour in range(3)]
    out_shape = []
    for width in widths:
        out_shape += [pltpu.HBM((8, rows, width), jnp.float32)] * 2
    flat = [array for pairs in operands for pair in pairs for array in pair]
    scratch = [pltpu.VMEM(array.shape, array.dtype) for array in flat]
    scratch += [pltpu.VMEM((height, sum(left.shape[0] for left, _ in pairs)), jnp.bfloat16) for pairs in operands]
    for colour in range(3):
        for ranges in parts:
            if ranges[colour][1]:
                scratch.append(pltpu.VMEM((height, ranges[colour][1]), jnp.float32))
    flops = sum(2 * left.size * right.shape[1] for pairs in operands for left, right in pairs)
    moved = sum(2 * array.size for array in flat) + sum(4 * 16 * rows * width for width in widths)
    return pl.pallas_call(
        functools.partial(grad_kernel, [(ranges, len(pairs)) for ranges, pairs in zip(parts, operands)], rows),
        out_shape=tuple(out_shape),
        in_specs=[pl.BlockSpec(memory_space=pltpu.SMEM)] + [pl.BlockSpec(memory_space=pltpu.HBM)] * len(flat),
        out_specs=tuple([pl.BlockSpec(memory_space=pltpu.HBM)] * 6),
        scratch_shapes=scratch + [pltpu.SemaphoreType.DMA((len(flat),)), pltpu.SemaphoreType.DMA((3,))],
        compiler_params=pltpu.CompilerParams(vmem_limit_bytes=30 * MEGA),
        cost_estimate=pl.CostEstimate(flops=flops, bytes_accessed=moved, transcendentals=0),
        name="weight_grads",
    )(here, *[in_hbm(array) for array in flat])


def combine_kernel(low, count, plan, *refs):
    terms = [term for group in plan for sums, _ in group for term in sums]
    sources = refs[: 1 + max(index for index, _ in terms)]
    outs = refs[len(sources) : len(sources) + len(plan)]
    places = list(refs[len(sources) + len(plan) : -2])
    in_sems, out_sems = refs[-2:]
    arriving = []
    for group in plan:
        for sums, width in group:
            for index, column in sums:
                source = sources[index].at[pl.ds(low, count), :, pl.ds(column, width)]
                arriving.append(Arriving(source, places.pop(0), in_sems.at[len(arriving)]))
    leaving = []
    for group, out in zip(plan, outs):
        place = places.pop(0)
        column = 0
        for sums, width in group:
            total = None
            for _ in sums:
                piece = arriving.pop(0)[...]
                total = piece if total is None else total + piece
            place[:, :, column : column + width] = total
            column += width
        leaving.append(Leaving(place, out, out_sems.at[len(leaving)]))
        leaving[-1].send()
    for view in leaving:
        view.finish()


def combine(state, low, count, groups):
    arrays, plan = [], []
    for group in groups:
        plan.append([])
        for colour in group:
            sums = []
            for array, column in state["terms"][colour]:
                known = [index for index, other in enumerate(arrays) if other is array]
                if not known:
                    arrays.append(array)
                sums.append((known[0] if known else len(arrays) - 1, column))
            plan[-1].append((sums, state["widths"][colour]))
    rows = arrays[0].shape[1]
    places = [
        pltpu.VMEM((count, rows, width), jnp.float32) for group in plan for sums, width in group for _ in sums
    ]
    results = [(count, rows, sum(width for _, width in group)) for group in plan]
    term_count = len(places)
    places += [pltpu.VMEM(shape, jnp.float32) for shape in results]
    return pl.pallas_call(
        functools.partial(combine_kernel, low, count, plan),
        out_shape=tuple(pltpu.HBM(shape, jnp.float32) for shape in results),
        in_specs=[pl.BlockSpec(memory_space=pltpu.HBM)] * len(arrays),
        out_specs=tuple([pl.BlockSpec(memory_space=pltpu.HBM)] * len(results)),
        scratch_shapes=places
        + [pltpu.SemaphoreType.DMA((term_count,)), pltpu.SemaphoreType.DMA((len(results),))],
        compiler_params=pltpu.CompilerParams(vmem_limit_bytes=16 * MEGA),
        cost_estimate=pl.CostEstimate(flops=1, bytes_accessed=1, transcendentals=0),
        name="combine",
    )(*[in_hbm(array) for array in arrays])


def scatter_groups(step):
    groups = []
    for colour, order in enumerate(ORDERS):
        for group in groups:
            if step >= 2 and set(ORDERS[group[0]][:step]) == set(order[:step]) and ORDERS[group[0]][step:] == order[step:]:
                group.append(colour)
                break
        else:
            groups.append([colour])
    return groups


def scatter_start(blocks, token):
    keeps = [blocks[2 * colour] for colour in range(3)]
    sends = [blocks[2 * colour + 1] for colour in range(3)]
    state = {"terms": [[(keep, 0)] for keep in keeps], "widths": [keep.shape[2] for keep in keeps], "half": 8, "step": 0}
    return state, scatter_send(state, sends, token)


def scatter_send(state, sends, token):
    sends, token = lax.optimization_barrier((list(sends), token))
    state["incoming"] = [
        lax.ppermute(send, "dp", [(i, i ^ ORDERS[colours[0]][state["step"]]) for i in range(16)])
        for send, colours in zip(sends, scatter_groups(state["step"]))
    ]
    return token


def scatter_next(state, token, *done):
    incoming, token, _ = lax.optimization_barrier((state["incoming"], token, done))
    for array, colours in zip(incoming, scatter_groups(state["step"])):
        column = 0
        for colour in colours:
            state["terms"][colour].append((array, column))
            column += state["widths"][colour]
    state["step"] += 1
    state["half"] //= 2
    if not state["half"]:
        return token
    return scatter_send(state, combine(state, state["half"], state["half"], scatter_groups(state["step"])), token)


def scatter_result(state, groups):
    return [result[0] for result in combine(state, 0, 1, groups)]


def all_sum(values):
    for mask in (STEP_X, STEP_Y, STEP_Z, STEP_W):
        values = values + lax.ppermute(values, "dp", [(i, i ^ mask) for i in range(16)])
    return values


def per_device(
    spread,
    hidden,
    lengths,
    spans,
    join_query,
    w_qkv,
    qv_bias,
    w_out,
    out_biases,
    norm_gains,
    norm_biases,
    w_up,
    up_bias,
    w_down,
    cotangent,
):
    row_count, seq, width = hidden.shape
    local = w_qkv.shape[2]
    units = w_up.shape[1]
    heads = local // HEAD
    rows = range(row_count)
    f32, bf16 = jnp.float32, jnp.bfloat16
    query_row = join_query.reshape(1, width)
    w_qkv_flat = w_qkv.reshape(width, 3 * local)
    qkv_bias = jnp.concatenate([qv_bias[0], jnp.zeros((local,), f32), qv_bias[1]]).reshape(1, 3 * local)
    up_bias_row = up_bias.reshape(1, units)
    log_rows = 8 * (-(-heads // 8))

    front = []
    for row in rows:
        front.append(
            run_kernel(
                functools.partial(front_kernel, row),
                "front",
                (
                    ((seq, width), f32),
                    ((seq, width), bf16),
                    ((seq, 3 * local), bf16),
                    ((seq, 128), f32),
                    ((log_rows, seq), f32),
                    ((seq, local), bf16),
                    ((seq, width), f32),
                ),
                ([hidden], spans, query_row, [w_qkv_flat], qkv_bias, [w_out]),
                (lengths,),
                row,
                flops=2 * seq * (2 * seq * width + 4 * width * local + 2 * seq * local),
            )
        )
    pooled, joined_low, qkv, stats, logs, context_low, attn_part = zip(*front)
    mid = []
    for row in rows:
        mid.append(
            run_kernel(
                mid_kernel,
                "mid",
                (
                    ((seq, width), f32),
                    ((seq, 1), f32),
                    ((seq, width), bf16),
                    ((seq, units), bf16),
                    ((seq, units), bf16),
                    ((seq, width), f32),
                ),
                (
                    (hidden,),
                    pooled[row],
                    attn_part[row],
                    [swap_cores(attn_part[row])],
                    out_biases,
                    norm_gains,
                    norm_biases,
                    [w_up],
                    up_bias_row,
                    [w_down],
                ),
                (),
                row,
                flops=4 * seq * width * units,
            )
        )
    normed, inv_std, first_low, act_low, slope, down_part = zip(*mid)
    turn = []
    for row in rows:
        turn.append(
            run_kernel(
                functools.partial(turn_kernel, row),
                "turn",
                (((seq, width), bf16), ((seq, width), f32), ((seq, width), bf16), ((8, width), f32)),
                (
                    normed[row],
                    down_part[row],
                    [swap_cores(down_part[row])],
                    (cotangent,),
                    out_biases,
                    norm_gains,
                    norm_biases,
                ),
                (lengths,),
                row,
                room=11,
                flops=seq * width,
            )
        )
    layer_out, d_down, d_down_low, turn_sums = zip(*turn)
    scattered = spread == 16 and width % 128 == 0
    token = lengths
    if scattered:
        here = lax.axis_index("dp").astype(jnp.int32).reshape(1)
        unit = units // 12
        down_cols = ((0, 5 * unit), (5 * unit, 4 * unit), (9 * unit, 3 * unit))
        up_cols = ((0, 4 * unit), (4 * unit, 5 * unit), (9 * unit, 3 * unit))
        out_cols = ((0, 0), (0, 0), (0, local))
        qkv_cols = ((0, 5 * local // 3), (5 * local // 3, 4 * local // 3), (0, 0))
        down_blocks = grad_blocks(here, [list(zip(d_down_low, act_low))], [down_cols])
        down_sum, token = scatter_start(down_blocks, token)
    ffn_back = run_kernel(
        functools.partial(units_kernel, row_count),
        "units",
        (((seq, units), bf16), ((seq, width), f32), ((1, units), f32)) * row_count,
        (w_down, w_up, *[array for pair in zip(d_down_low, slope) for array in pair]),
        (token,),
        flops=4 * row_count * seq * width * units,
    )
    d_up_low, back_part, up_sums = ffn_back[0::3], ffn_back[1::3], ffn_back[2::3]
    if scattered:
        token = scatter_next(down_sum, token, up_sums)
        back_part, token = lax.optimization_barrier((back_part, token))
        here, token = lax.optimization_barrier((here, token))
        up_blocks = grad_blocks(here, [list(zip(first_low, d_up_low))], [up_cols])
    back = []
    for row in rows:
        back.append(
            run_kernel(
                functools.partial(back_kernel, row),
                "back",
                (
                    ((seq, width), f32),
                    ((seq, width), bf16),
                    ((seq, 3 * local), bf16),
                    ((seq, width), f32),
                    ((8, width), f32),
                    ((2, local), f32),
                    ((seq, local), bf16),
                ),
                (
                    back_part[row],
                    [swap_cores(back_part[row])],
                    d_down[row],
                    normed[row],
                    inv_std[row],
                    norm_gains,
                    qkv[row],
                    logs[row],
                    [w_out],
                    [w_qkv_flat],
                ),
                (token,),
                flops=2 * seq * (4 * width * local + 5 * seq * local),
            )
        )
        if scattered and row == 0:
            token = scatter_next(down_sum, token, back[-1][4])
            up_sum, token = scatter_start(up_blocks, token)
    if scattered:
        token = scatter_next(up_sum, token, back[-1][4])
    d_attn, d_attn_low, d_proj, join_part, back_sums, qv_sums, _ = zip(*back)
    if scattered:
        here, token = lax.optimization_barrier((here, token))
        rest_blocks = grad_blocks(
            here, [list(zip(d_attn_low, context_low)), list(zip(joined_low, d_proj))], [out_cols, qkv_cols]
        )
        rest_blocks, token = lax.optimization_barrier((rest_blocks, token))
        token = scatter_next(up_sum, token)
        rest_sum, token = scatter_start(rest_blocks, token)
    joined_back = []
    for row in rows:
        joined_back.append(
            run_kernel(
                functools.partial(join_back_kernel, row, heads),
                "join_back",
                (((seq, width), f32), ((1, width), f32)),
                (
                    (hidden,),
                    spans,
                    query_row,
                    join_part[row],
                    [swap_cores(join_part[row])],
                    d_attn[row],
                    pooled[row],
                    stats[row],
                ),
                (token,),
                row,
                room=17,
                flops=4 * seq * seq * width,
            )
        )
    grad_inputs, join_grads = zip(*joined_back)
    join_grad = sum(join_grads[1:], join_grads[0])
    turn_sum = sum(turn_sums[1:], turn_sums[0])
    back_sum = sum(back_sums[1:], back_sums[0])
    small = (
        sum(qv_sums[1:], qv_sums[0]),
        sum(up_sums[1:], up_sums[0]).reshape(units),
        jnp.stack([back_sum[2], turn_sum[2]]),
        jnp.stack([back_sum[0], turn_sum[0]]),
        jnp.stack([back_sum[1], turn_sum[1]]),
        join_grad.reshape(width),
    )
    if scattered:
        token = scatter_next(rest_sum, token, join_grad)
        token = scatter_next(up_sum, token)
        token = scatter_next(rest_sum, token)
        token = scatter_next(down_sum, token)
        token = scatter_next(rest_sum, token)
        token = scatter_next(rest_sum, token)
        token = scatter_next(up_sum, token)
        token = scatter_next(down_sum, token)
        (down_rows,) = scatter_result(down_sum, [[0, 1, 2]])
        (up_rows,) = scatter_result(up_sum, [[0, 1, 2]])
        qkv_rows, out_rows = scatter_result(rest_sum, [[0, 1], [2]])
        qkv_rows = qkv_rows.reshape(-1, 3, local)
        sizes = [math.prod(value.shape) for value in small]
        packed = all_sum(jnp.concatenate([value.reshape(-1) for value in small]).reshape(-1, 128)).reshape(-1)
        summed, offset = [], 0
        for value, size in zip(small, sizes):
            summed.append(packed[offset : offset + size].reshape(value.shape))
            offset += size
    else:

        def first_product(lefts, rights):
            total = sum(dot(left, right, TN) for left, right in zip(lefts, rights))
            return lax.psum_scatter(total, "dp", scatter_dimension=0, tiled=True)

        down_rows = first_product(d_down_low, act_low)
        up_rows = first_product(first_low, d_up_low)
        out_rows = first_product(d_attn_low, context_low)
        qkv_rows = first_product(joined_low, d_proj).reshape(-1, 3, local)
        summed = lax.psum(small, "dp")
    return (
        jnp.stack(layer_out),
        jnp.stack(grad_inputs),
        qkv_rows,
        summed[0],
        out_rows,
        summed[2],
        summed[3],
        summed[4],
        up_rows,
        summed[1],
        down_rows,
        summed[5],
    )


def solution(mesh):
    return jax.shard_map(
        functools.partial(per_device, mesh.shape["dp"]),
        mesh=mesh,
        in_specs=(
            P("dp", None, None),
            P("dp"),
            P("dp", None),
            P(),
            P(None, None, "tensor"),
            P(None, "tensor"),
            P(None, "tensor"),
            P(),
            P(),
            P(),
            P(None, "tensor"),
            P("tensor"),
            P(None, "tensor"),
            P("dp", None, None),
        ),
        out_specs=(
            P("dp", None, None),
            P("dp", None, None),
            P("dp", None, "tensor"),
            P(None, "tensor"),
            P("dp", "tensor"),
            P(),
            P(),
            P(),
            P("dp", "tensor"),
            P("tensor"),
            P("dp", "tensor"),
            P(),
        ),
        check_vma=False,
    )
```

```python
import functools
import math

import jax
import jax.numpy as jnp
from jax import lax
from jax.experimental import pallas as pl
from jax.experimental.pallas import tpu as pltpu
from jax.sharding import PartitionSpec as P

HEAD = 64


EPS = 1e-05
NEGATIVE = -1e30
MEGA = 1024 * 1024
SMALL = 64 * 1024
SMALL_ROWS = 16


def swap_cores(part):
    return lax.ppermute(part, "tensor", [(0, 1), (1, 0)])


STEP_X, STEP_Y, STEP_Z, STEP_W = 1, 2, 4, 12
ORDERS = (
    (STEP_X, STEP_Y, STEP_Z, STEP_W),
    (STEP_Y, STEP_Z, STEP_X, STEP_W),
    (STEP_Z, STEP_X, STEP_Y, STEP_W),
)


def relative_block(order, place):
    steps = len(order)
    block = 0
    for position, mask in enumerate(order):
        if (place >> (steps - 1 - position)) & 1:
            block ^= mask
    return block


def dot(left, right, contract=((1,), (0,))):
    return lax.dot_general(left, right, (contract, ((), ())), preferred_element_type=jnp.float32)


NT = ((1,), (1,))
TN = ((0,), (0,))


class Arriving:
    def __init__(self, source, place, sem):
        self.copy, self.place, self.shape, self.waited = pltpu.make_async_copy(source, place, sem), place, place.shape, False
        self.copy.start()

    def ready(self):
        if not self.waited:
            self.copy.wait()
            self.waited = True
        return self.place

    def __getitem__(self, index):
        return self.ready()[index]


class Leaving:
    def __init__(self, place, target, sem):
        self.place, self.target, self.sem, self.shape, self.copies = place, target, sem, place.shape, []

    def __getitem__(self, index):
        return self.place[index]

    def __setitem__(self, index, value):
        self.place[index] = value

    def send(self, rows=slice(None), columns=slice(None)):
        source, target = self.place.at[rows, columns], self.target.at[rows, columns]
        self.copies.append(pltpu.make_async_copy(source, target, self.sem))
        self.copies[-1].start()

    def finish(self):
        if not self.copies:
            self.send()
        for copy in self.copies:
            copy.wait()


def moving_kernel(body, row, flags, scalar_count, *refs):
    count = len(flags)
    scalars, arrays, rest = refs[:scalar_count], refs[scalar_count : scalar_count + count], list(refs[scalar_count + count :])
    sems = rest.pop()
    views, leaving = [], []
    for index, (flag, array) in enumerate(zip(flags, arrays)):
        if flag == "small":
            views.append(array)
        elif flag == "out":
            views.append(Leaving(rest.pop(0), array, sems.at[index]))
            leaving.append(views[-1])
        else:
            source = array.at[row] if flag == "row" else array
            views.append(Arriving(source, rest.pop(0), sems.at[index]))
    body(*scalars, *views)
    for view in views:
        if isinstance(view, Arriving):
            view.ready()
    for view in leaving:
        view.finish()


def in_hbm(array):
    return pltpu.with_memory_space_constraint(array, pltpu.HBM)


def in_vmem(array):
    return pltpu.with_memory_space_constraint(array, pltpu.VMEM)


def run_kernel(body, name, outputs, operands, scalars=(), row=None, flops=0, room=12):
    flags, arrays, places, specs = [], [], [], []
    small_spec, large_spec = pl.BlockSpec(memory_space=pltpu.VMEM), pl.BlockSpec(memory_space=pltpu.HBM)
    for operand in operands:
        by_row, placed = isinstance(operand, tuple), isinstance(operand, list)
        array = operand[0] if by_row or placed else operand
        small = placed or array.size < SMALL
        arrays.append(in_vmem(array) if placed else array if small else in_hbm(array))
        flags.append("small" if small else "row" if by_row else "whole")
        specs.append(small_spec if small else large_spec)
        if not small:
            places.append(pltpu.VMEM(array.shape[1:] if by_row else array.shape, array.dtype))
    out_specs, out_shapes = [], []
    for shape, dtype in outputs:
        small = math.prod(shape) < SMALL
        flags.append("small" if small else "out")
        out_specs.append(small_spec if small else large_spec)
        out_shapes.append(jax.ShapeDtypeStruct(shape, dtype) if small else pltpu.HBM(shape, dtype))
        if not small:
            places.append(pltpu.VMEM(shape, dtype))
    held = sum(math.prod(place.shape) * jnp.dtype(place.dtype).itemsize for place in places)
    return pl.pallas_call(
        functools.partial(moving_kernel, body, row, flags, len(scalars)),
        out_shape=tuple(out_shapes),
        in_specs=[pl.BlockSpec(memory_space=pltpu.SMEM)] * len(scalars) + specs,
        out_specs=tuple(out_specs),
        scratch_shapes=places + [pltpu.SemaphoreType.DMA((len(flags),))],
        compiler_params=pltpu.CompilerParams(vmem_limit_bytes=held + room * MEGA),
        cost_estimate=pl.CostEstimate(flops=flops, bytes_accessed=held, transcendentals=0),
        name=name,
    )(*scalars, *arrays)


def square_iota(size):
    return lax.broadcasted_iota(jnp.int32, (size, size), 0), lax.broadcasted_iota(jnp.int32, (size, size), 1)


def halves(values):
    high = values.astype(jnp.bfloat16)
    return high, (values - high.astype(jnp.float32)).astype(jnp.bfloat16)


def same_span(spans_ref, row):
    span_row = spans_ref[row : row + 1, :].astype(jnp.float32)
    down, along = square_iota(span_row.shape[1])
    eye = down == along
    span_col = jnp.sum(jnp.where(eye, span_row, 0.0), 1, keepdims=True)
    return span_col == span_row, eye


def head_masks():
    lane = lax.broadcasted_iota(jnp.int32, (1, 2 * HEAD), 1)
    first = (lane < HEAD).astype(jnp.float32).astype(jnp.bfloat16)
    second = (lane >= HEAD).astype(jnp.float32).astype(jnp.bfloat16)
    return first, second


def pair_lanes(pair, start):
    return pl.ds(pl.multiple_of(start + pair * 2 * HEAD, 2 * HEAD), 2 * HEAD)


def norm_rows(resid):
    centered = resid - jnp.mean(resid, -1, keepdims=True)
    inv_std = lax.rsqrt(jnp.mean(centered * centered, -1, keepdims=True) + EPS)
    return centered * inv_std, inv_std


def norm_back(grad_in, gain_vec, normed, inv_std):
    d_normed = grad_in * gain_vec
    return inv_std * (
        d_normed
        - jnp.mean(d_normed, -1, keepdims=True)
        - normed * jnp.mean(d_normed * normed, -1, keepdims=True)
    )


def front_kernel(row, lengths_ref, hidden_ref, spans_ref, query_ref, w_qkv_ref, bias_ref, w_out_ref, *outs):
    pooled_ref, low_ref, qkv_ref, stats_ref, logs_ref, context_ref, part_ref = outs
    hidden = hidden_ref[row]
    seq, width = hidden.shape
    local = context_ref.shape[1]
    heads = local // HEAD
    inputs = hidden.astype(jnp.float32)
    score = jnp.sum(inputs * query_ref[...], 1, keepdims=True)
    same, eye = same_span(spans_ref, row)
    score_row = jnp.sum(jnp.where(eye, score, 0.0), 0, keepdims=True)
    top_row = jnp.max(jnp.where(same, score, NEGATIVE), 0, keepdims=True)
    weight_row = jnp.exp(score_row - top_row)
    weight = jnp.sum(jnp.where(eye, weight_row, 0.0), 1, keepdims=True)
    spread = jnp.where(same, weight_row, 0.0)
    total = jnp.sum(spread, 1, keepdims=True)
    high, low = halves(spread)
    pooled = (dot(high, hidden) + dot(low, hidden)) / total
    pooled_ref[...] = pooled
    pooled_ref.send()
    low_ref[...] = (inputs + pooled).astype(jnp.bfloat16)
    low_ref.send()
    lane = lax.broadcasted_iota(jnp.int32, (1, 128), 1)
    stats_ref[...] = jnp.where(lane == heads, total, jnp.where(lane == heads + 1, weight, 0.0))
    for part in range(3):
        columns = slice(part * local, (part + 1) * local)
        proj = dot(low_ref[...], w_qkv_ref[part]) + bias_ref[:, columns]
        if part == 0:
            proj = proj * (1.0 / math.sqrt(HEAD))
        qkv_ref[:, columns] = proj.astype(jnp.bfloat16)
    qkv_ref.send()
    valid = lax.broadcasted_iota(jnp.int32, (1, seq), 1) < lengths_ref[row]
    masks = head_masks()
    block = seq // 2

    def attend(pair, carry):
        query = qkv_ref[:, pair_lanes(pair, 0)]
        key = qkv_ref[:, pair_lanes(pair, local)]
        value = qkv_ref[:, pair_lanes(pair, 2 * local)]
        for step in range(2):
            rows = slice(step * block, (step + 1) * block)
            context = None
            stats = stats_ref[rows, :]
            for half in range(2):
                scores = dot(query[rows] * masks[half], key, NT)
                scores = jnp.where(valid, scores, NEGATIVE)
                top = jnp.max(scores, -1, keepdims=True)
                expo = jnp.exp(scores - top)
                expo_sum = jnp.sum(expo, -1, keepdims=True)
                probs = (expo * (1.0 / expo_sum)).astype(jnp.bfloat16)
                piece = dot(probs, value * masks[half])
                context = piece if context is None else context + piece
                stats = jnp.where(lane == 2 * pair + half, top + jnp.log(expo_sum), stats)
            stats_ref[rows, :] = stats
            context_ref[rows, pair_lanes(pair, 0)] = context.astype(jnp.bfloat16)
        return carry

    lax.fori_loop(0, heads // 2, attend, 0)
    context_ref.send()
    logs_ref[...] = jnp.transpose(stats_ref[...])[: logs_ref.shape[0]]
    for rows in (slice(0, block), slice(block, seq)):
        part_ref[rows, :] = dot(context_ref[rows, :], w_out_ref[...], NT)
        part_ref.send(rows=rows)


def mid_kernel(hidden_ref, pooled_ref, part_ref, other_ref, biases_ref, gains_ref, shifts_ref, w_up_ref, up_bias_ref, w_down_ref, *outs):
    normed_ref, inv_ref, low_ref, act_ref, slope_ref, down_ref = outs
    resid = hidden_ref[...].astype(jnp.float32) + pooled_ref[...]
    resid = resid + ((part_ref[...] + other_ref[...]) + biases_ref[0:1, :])
    normed, inv_std = norm_rows(resid)
    normed_ref[...] = normed
    normed_ref.send()
    inv_ref[...] = inv_std
    low_ref[...] = (normed * gains_ref[0:1, :] + shifts_ref[0:1, :]).astype(jnp.bfloat16)
    low_ref.send()
    chunk, step = 256, 64
    total = None
    for start in range(0, act_ref.shape[1], chunk):
        columns = slice(start, start + chunk)
        up = dot(low_ref[...], w_up_ref[:, columns]) + up_bias_ref[:, columns]
        for first in range(0, up.shape[0], step):
            rows = slice(first, first + step)
            piece = up[rows]
            cdf = 0.5 * (1.0 + lax.erf(piece * math.sqrt(0.5)))
            density = jnp.exp(piece * piece * -0.5) * (1.0 / math.sqrt(2.0 * math.pi))
            act_ref[rows, columns] = (piece * cdf).astype(jnp.bfloat16)
            slope_ref[rows, columns] = (cdf + piece * density).astype(jnp.bfloat16)
        down = dot(act_ref[:, columns], w_down_ref[:, columns], NT)
        total = down if total is None else total + down
        if start % (2 * chunk):
            act_ref.send(columns=slice(start - chunk, start + chunk))
            slope_ref.send(columns=slice(start - chunk, start + chunk))
    down_ref[...] = total


def turn_kernel(row, lengths_ref, normed_ref, down_ref, other_ref, cotangent_ref, biases_ref, gains_ref, shifts_ref, *outs):
    out_ref, d_down_ref, d_down_low_ref, sums_ref = outs
    seq = normed_ref.shape[0]
    first_norm = normed_ref[...] * gains_ref[0:1, :] + shifts_ref[0:1, :]
    normed, inv_std = norm_rows(first_norm + ((down_ref[...] + other_ref[...]) + biases_ref[1:2, :]))
    out_ref[...] = (normed * gains_ref[1:2, :] + shifts_ref[1:2, :]).astype(jnp.bfloat16)
    valid = (lax.broadcasted_iota(jnp.int32, (seq, 1), 0) < lengths_ref[row]).astype(jnp.float32)
    out_ref.send()
    d_out = cotangent_ref[...].astype(jnp.float32) * valid
    sums_ref[0:1, :] = jnp.sum(d_out * normed, 0, keepdims=True)
    sums_ref[1:2, :] = jnp.sum(d_out, 0, keepdims=True)
    d_down = norm_back(d_out, gains_ref[1:2, :], normed, inv_std)
    sums_ref[2:3, :] = jnp.sum(d_down, 0, keepdims=True)
    sums_ref[3:8, :] = jnp.zeros((5, sums_ref.shape[1]), jnp.float32)
    d_down_ref[...] = d_down
    d_down_low_ref[...] = d_down.astype(jnp.bfloat16)


def units_kernel(rows, token_ref, w_down_ref, w_up_ref, *refs):
    for row in range(rows):
        d_down_low_ref, slope_ref = refs[2 * row : 2 * row + 2]
        d_up_ref, up_sums_ref = refs[2 * rows + 2 * row : 2 * rows + 2 + 2 * row]
        back_ref = refs[4 * rows]
        chunk = 256
        total = None
        for start in range(0, d_up_ref.shape[1], chunk):
            columns = slice(start, start + chunk)
            d_up = dot(d_down_low_ref[...], w_down_ref[:, columns]) * slope_ref[:, columns].astype(jnp.float32)
            up_sums_ref[:, columns] = jnp.sum(d_up, 0, keepdims=True)
            d_up_ref[:, columns] = d_up.astype(jnp.bfloat16)
            back = dot(d_up_ref[:, columns], w_up_ref[:, columns], NT)
            total = back if total is None else total + back
            if start % (2 * chunk):
                d_up_ref.send(columns=slice(start - chunk, start + chunk))
        back_ref[row] = total
        back_ref.send(row)


def back_kernel(rows, lengths_ref, back_ref, other_ref, gains_ref, w_out_ref, w_qkv_ref, *refs):
    for row in range(rows):
        operands = refs[5 * row : 5 * row + 5]
        outs = refs[5 * rows + 6 * row : 5 * rows + 6 * row + 6]
        back_row(row, lengths_ref, back_ref, other_ref, gains_ref, w_out_ref, w_qkv_ref, *operands, *outs, refs[-1])


def back_row(row, lengths_ref, back_ref, other_ref, gains_ref, w_out_ref, w_qkv_ref, *refs):
    d_down_ref, normed_ref, inv_ref, qkv_ref, logs_ref = refs[:5]
    d_attn_ref, d_attn_low_ref, d_proj_ref, sums_ref, qv_sums_ref, d_context_ref, join_ref = refs[5:]
    seq = normed_ref.shape[0]
    local = d_context_ref.shape[1]
    normed = normed_ref[...]
    d_first = (back_ref[row] + other_ref[row]) + d_down_ref[...]
    sums_ref[0:1, :] = jnp.sum(d_first * normed, 0, keepdims=True)
    sums_ref[1:2, :] = jnp.sum(d_first, 0, keepdims=True)
    d_attn = norm_back(d_first, gains_ref[0:1, :], normed, inv_ref[...])
    sums_ref[2:3, :] = jnp.sum(d_attn, 0, keepdims=True)
    sums_ref[3:8, :] = jnp.zeros((5, sums_ref.shape[1]), jnp.float32)
    d_attn_ref[...] = d_attn
    d_attn_ref.send()
    d_attn_low_ref[...] = d_attn.astype(jnp.bfloat16)
    d_attn_low_ref.send()
    d_context_ref[...] = dot(d_attn_low_ref[...], w_out_ref[...]).astype(jnp.bfloat16)
    qkv_ref.ready()
    scale = 1.0 / math.sqrt(HEAD)
    masks = head_masks()
    block = seq // 2
    valid = lax.broadcasted_iota(jnp.int32, (seq, 1), 0) < lengths_ref[row]

    def attend(pair, carry):
        query = qkv_ref[:, pair_lanes(pair, 0)]
        key = qkv_ref[:, pair_lanes(pair, local)]
        value = qkv_ref[:, pair_lanes(pair, 2 * local)]
        grad = d_context_ref[:, pair_lanes(pair, 0)]
        d_key = d_value = None
        query_sum = jnp.zeros((1, 2 * HEAD), jnp.float32)
        for step in range(2):
            columns = slice(step * block, (step + 1) * block)
            d_query = None
            for half in range(2):
                query_part = query[columns] * masks[half]
                grad_part = grad[columns] * masks[half]
                scores = jnp.where(valid, dot(key, query_part, NT), NEGATIVE)
                probs = jnp.exp(scores - logs_ref[pl.ds(2 * pair + half, 1), columns])
                d_probs = dot(value, grad_part, NT)
                piece = dot(probs.astype(jnp.bfloat16), grad_part)
                d_value = piece if d_value is None else d_value + piece
                d_scores = probs * (d_probs - jnp.sum(d_probs * probs, 0, keepdims=True))
                d_scores = d_scores.astype(jnp.bfloat16)
                piece = dot(d_scores, query_part)
                d_key = piece if d_key is None else d_key + piece
                piece = dot(d_scores, key * masks[half], TN)
                d_query = piece if d_query is None else d_query + piece
            d_query = d_query * scale
            query_sum = query_sum + jnp.sum(d_query, 0, keepdims=True)
            d_proj_ref[columns, pair_lanes(pair, 0)] = d_query.astype(jnp.bfloat16)
        d_proj_ref[:, pair_lanes(pair, local)] = d_key.astype(jnp.bfloat16)
        d_proj_ref[:, pair_lanes(pair, 2 * local)] = d_value.astype(jnp.bfloat16)
        qv_sums_ref[0:1, pair_lanes(pair, 0)] = query_sum
        qv_sums_ref[1:2, pair_lanes(pair, 0)] = jnp.sum(d_value, 0, keepdims=True)
        return carry

    lax.fori_loop(0, local // (2 * HEAD), attend, 0)
    d_proj_ref.send()
    total = None
    for part in range(3):
        piece = dot(d_proj_ref[:, part * local : (part + 1) * local], w_qkv_ref[part], NT)
        total = piece if total is None else total + piece
    join_ref[row] = total
    join_ref.send(row)


def join_back_kernel(rows, heads, lengths_ref, hidden_ref, spans_ref, query_ref, join_ref, other_ref, *refs):
    grad_ref, sums_ref = refs[3 * rows :]
    for row in range(rows):
        join_back_row(row, heads, hidden_ref, spans_ref, query_ref, join_ref, other_ref, *refs[3 * row : 3 * row + 3], grad_ref, sums_ref)


def join_back_row(row, heads, hidden_ref, spans_ref, query_ref, join_ref, other_ref, d_attn_ref, pooled_ref, stats_ref, grad_ref, sums_ref):
    total = stats_ref[:, heads : heads + 1]
    weight = stats_ref[:, heads + 1 : heads + 2]
    d_joined = (join_ref[row] + other_ref[row]) + d_attn_ref[...]
    d_total = -jnp.sum(d_joined * pooled_ref[...], 1, keepdims=True) / total
    same, eye = same_span(spans_ref, row)
    d_total_row = jnp.sum(jnp.where(eye, d_total, 0.0), 0, keepdims=True)
    high, low = halves(d_joined / total)
    chosen = same.astype(jnp.float32).astype(jnp.bfloat16)
    d_weighted = dot(chosen, high) + dot(chosen, low)
    inputs = hidden_ref[row].astype(jnp.float32)
    d_weight = jnp.sum(jnp.where(same, d_total_row, 0.0), 1, keepdims=True)
    d_weight = d_weight + jnp.sum(d_weighted * inputs, 1, keepdims=True)
    d_score = weight * d_weight
    grad_ref[row] = d_joined + weight * d_weighted + d_score * query_ref[...]
    grad_ref.send(row)
    sums_ref[row : row + 1, :] = jnp.sum(d_score * inputs, 0, keepdims=True)


def grad_kernel(parts, rows, *refs):
    here_ref = refs[0]
    count = sum(2 * terms for _, terms in parts)
    sources = refs[1 : 1 + count]
    outs = refs[1 + count : 7 + count]
    places = refs[7 + count : 7 + 2 * count]
    turned = refs[7 + 2 * count : 7 + 2 * count + len(parts)]
    totals = refs[7 + 2 * count + len(parts) : -2]
    in_sems, sem = refs[-2:]
    here = here_ref[0]
    order_in = list(range(0, count, 2)) + list(range(1, count, 2))
    operands = {index: Arriving(sources[index], places[index], in_sems.at[index]) for index in order_in}
    copies = []
    first = 0
    for part, (_, terms) in enumerate(parts):
        for term in range(terms):
            left = operands[first + 2 * term]
            size = left.shape[0]
            turned[part][:, term * size : (term + 1) * size] = jnp.transpose(left[...])
        first += 2 * terms
    slot = 0
    for colour, order in enumerate(ORDERS):
        column = first = 0
        for part, (ranges, terms) in enumerate(parts):
            start, width = ranges[colour]
            if width:
                total = totals[slot]
                slot += 1
                product = None
                for term in range(terms):
                    right = operands[first + 2 * term + 1]
                    size = right.shape[0]
                    left = turned[part][:, term * size : (term + 1) * size]
                    piece = dot(left, right[:, start : start + width])
                    product = piece if product is None else product + piece
                total[...] = product
                for place in range(16):
                    block = jnp.bitwise_xor(here, relative_block(order, place))
                    source = total.at[pl.ds(pl.multiple_of(block * rows, 8), rows), :]
                    target = outs[2 * colour + place // 8].at[place % 8, :, pl.ds(column, width)]
                    copy = pltpu.make_async_copy(source, target, sem.at[colour])
                    copy.start()
                    copies.append(copy)
                column += width
            first += 2 * terms
    for copy in copies:
        copy.wait()


def grad_blocks(here, operands, parts):
    height = operands[0][0][0].shape[1]
    rows = height // 16
    widths = [sum(ranges[colour][1] for ranges in parts) for colour in range(3)]
    out_shape = []
    for width in widths:
        out_shape += [pltpu.HBM((8, rows, width), jnp.float32)] * 2
    flat = [array for pairs in operands for pair in pairs for array in pair]
    scratch = [pltpu.VMEM(array.shape, array.dtype) for array in flat]
    scratch += [pltpu.VMEM((height, sum(left.shape[0] for left, _ in pairs)), jnp.bfloat16) for pairs in operands]
    for colour in range(3):
        for ranges in parts:
            if ranges[colour][1]:
                scratch.append(pltpu.VMEM((height, ranges[colour][1]), jnp.float32))
    flops = sum(2 * left.size * right.shape[1] for pairs in operands for left, right in pairs)
    moved = sum(2 * array.size for array in flat) + sum(4 * 16 * rows * width for width in widths)
    return pl.pallas_call(
        functools.partial(grad_kernel, [(ranges, len(pairs)) for ranges, pairs in zip(parts, operands)], rows),
        out_shape=tuple(out_shape),
        in_specs=[pl.BlockSpec(memory_space=pltpu.SMEM)] + [pl.BlockSpec(memory_space=pltpu.HBM)] * len(flat),
        out_specs=tuple([pl.BlockSpec(memory_space=pltpu.HBM)] * 6),
        scratch_shapes=scratch + [pltpu.SemaphoreType.DMA((len(flat),)), pltpu.SemaphoreType.DMA((3,))],
        compiler_params=pltpu.CompilerParams(vmem_limit_bytes=30 * MEGA),
        cost_estimate=pl.CostEstimate(flops=flops, bytes_accessed=moved, transcendentals=0),
        name="weight_grads",
    )(here, *[in_hbm(array) for array in flat])


def combine_kernel(low, count, source_count, plan, extra, *refs):
    sources = refs[:source_count]
    out_count = len(plan) + (1 if extra and not low else 0)
    outs = refs[source_count : source_count + out_count]
    places = list(refs[source_count + out_count : -2])
    in_sems, out_sems = refs[-2:]
    arriving, small = [], []
    for group in plan:
        for sums, width in group:
            for index, column in sums:
                place = places.pop(0)
                rows = place.shape[1]
                source = sources[index].at[pl.ds(low, count), pl.ds(0, rows), pl.ds(column, width)]
                arriving.append(Arriving(source, place, in_sems.at[len(arriving)]))
    for index, block, row in extra:
        place = places.pop(0)
        source = sources[index].at[block, pl.ds(row, place.shape[0]), pl.ds(0, place.shape[1])]
        small.append(Arriving(source, place, in_sems.at[len(arriving) + len(small)]))
    leaving = []
    small_total = None
    for group, out in zip(plan, outs):
        place = places.pop(0)
        column = 0
        for sums, width in group:
            total = None
            for _ in sums:
                piece = arriving.pop(0)[...]
                total = piece if total is None else total + piece
            place[:count, :rows, column : column + width] = total
            column += width
        if extra and small_total is None:
            for view in small:
                small_total = view[...] if small_total is None else small_total + view[...]
            high, wide = small_total.shape
            if place.shape[0] > count:
                place[count] = jnp.zeros(place.shape[1:], jnp.float32)
                place[count, :high, :wide] = small_total
            elif place.shape[1] > rows:
                place[0, rows:, :] = jnp.zeros((high, place.shape[2]), jnp.float32)
                place[0, rows:, :wide] = small_total
        leaving.append(Leaving(place, out, out_sems.at[len(leaving)]))
        leaving[-1].send()
    if out_count > len(plan):
        place = places.pop(0)
        place[...] = small_total
        leaving.append(Leaving(place, outs[-1], out_sems.at[len(leaving)]))
    for view in leaving:
        view.finish()


def combine(state, low, count, groups):
    arrays, plan = [], []

    def number(array):
        for index, other in enumerate(arrays):
            if other is array:
                return index
        arrays.append(array)
        return len(arrays) - 1

    for group in groups:
        plan.append([])
        for piece in group:
            colour, start, width = piece if isinstance(piece, tuple) else (piece, 0, state["widths"][piece])
            plan[-1].append(([(number(array), column + start) for array, column in state["terms"][colour]], width))
    extra = [(number(array), block, row) for array, block, row in state["extra"]]
    rows = state["rows"]
    places = [
        pltpu.VMEM((count, rows, width), jnp.float32) for group in plan for sums, width in group for _ in sums
    ]
    small_shape = (SMALL_ROWS, state["widths"][0])
    places += [pltpu.VMEM(small_shape, jnp.float32) for _ in extra]
    term_count = len(places)
    results = [(count, rows, sum(width for _, width in group)) for group in plan]
    if extra and not low:
        results.append(small_shape)
    elif extra and len(groups) > 1:
        results[0] = (count + 1, *results[0][1:])
    elif extra:
        results[0] = (count, rows + SMALL_ROWS, results[0][2])
    places += [pltpu.VMEM(shape, jnp.float32) for shape in results]
    return pl.pallas_call(
        functools.partial(combine_kernel, low, count, len(arrays), plan, extra),
        out_shape=tuple(pltpu.HBM(shape, jnp.float32) for shape in results),
        in_specs=[pl.BlockSpec(memory_space=pltpu.HBM)] * len(arrays),
        out_specs=tuple([pl.BlockSpec(memory_space=pltpu.HBM)] * len(results)),
        scratch_shapes=places
        + [pltpu.SemaphoreType.DMA((term_count,)), pltpu.SemaphoreType.DMA((len(results),))],
        compiler_params=pltpu.CompilerParams(vmem_limit_bytes=16 * MEGA),
        cost_estimate=pl.CostEstimate(flops=1, bytes_accessed=1, transcendentals=0),
        name="combine",
    )(*[in_hbm(array) for array in arrays])


def scatter_groups(step):
    groups = []
    for colour, order in enumerate(ORDERS):
        for group in groups:
            if step >= 2 and set(ORDERS[group[0]][:step]) == set(order[:step]) and ORDERS[group[0]][step:] == order[step:]:
                group.append(colour)
                break
        else:
            groups.append([colour])
    return groups


def scatter_start(blocks, token):
    keeps = [blocks[2 * colour] for colour in range(3)]
    sends = [blocks[2 * colour + 1] for colour in range(3)]
    state = {"terms": [[(keep, 0)] for keep in keeps], "widths": [keep.shape[2] for keep in keeps], "half": 8, "step": 0}
    state.update(sends=sends, extra=[], rows=keeps[0].shape[1])
    return state, scatter_send(state, token)


def scatter_send(state, token):
    sends, token = lax.optimization_barrier((list(state["sends"]), token))
    state["incoming"] = [
        lax.ppermute(send, "dp", [(i, i ^ ORDERS[colours[0]][state["step"]]) for i in range(16)])
        for send, colours in zip(sends, scatter_groups(state["step"]))
    ]
    return token


def scatter_receive(state, token, *done, small=None):
    incoming, token, _ = lax.optimization_barrier((state["incoming"], token, done))
    for array, colours in zip(incoming, scatter_groups(state["step"])):
        column = 0
        for colour in colours:
            state["terms"][colour].append((array, column))
            column += state["widths"][colour]
    if state["extra"] and state["step"]:
        merged = len(incoming) == 1
        state["extra"].append((incoming[0], 0 if merged else state["half"], state["rows"] if merged else 0))
    if small is not None:
        state["extra"] = [(small, 0, 0)]
    state["step"] += 1
    state["half"] //= 2
    if state["half"]:
        sends = combine(state, state["half"], state["half"], scatter_groups(state["step"]))
        state["sends"], token = lax.optimization_barrier((sends, token))
    return token


def scatter_next(state, token, *done, small=None):
    return scatter_send(state, scatter_receive(state, token, *done, small=small))


def scatter_result(state, groups):
    results = combine(state, 0, 1, groups)
    return [result[0] for result in results[: len(groups)]] + list(results[len(groups) :])


def sum_step(values, mask, token):
    values, token = lax.optimization_barrier((values, token))
    return values + lax.ppermute(values, "dp", [(i, i ^ mask) for i in range(16)])


def per_device(
    spread,
    hidden,
    lengths,
    spans,
    join_query,
    w_qkv,
    qv_bias,
    w_out,
    out_biases,
    norm_gains,
    norm_biases,
    w_up,
    up_bias,
    w_down,
    cotangent,
):
    row_count, seq, width = hidden.shape
    local = w_qkv.shape[2]
    units = w_up.shape[1]
    heads = local // HEAD
    rows = range(row_count)
    f32, bf16 = jnp.float32, jnp.bfloat16
    query_row = join_query.reshape(1, width)
    w_parts = jnp.transpose(w_qkv, (1, 0, 2))
    qkv_bias = jnp.concatenate([qv_bias[0], jnp.zeros((local,), f32), qv_bias[1]]).reshape(1, 3 * local)
    up_bias_row = up_bias.reshape(1, units)
    log_rows = 8 * (-(-heads // 8))

    front = []
    for row in rows:
        front.append(
            run_kernel(
                functools.partial(front_kernel, row),
                "front",
                (
                    ((seq, width), f32),
                    ((seq, width), bf16),
                    ((seq, 3 * local), bf16),
                    ((seq, 128), f32),
                    ((log_rows, seq), f32),
                    ((seq, local), bf16),
                    ((seq, width), f32),
                ),
                ([hidden], spans, query_row, [w_parts], qkv_bias, [w_out]),
                (lengths,),
                row,
                flops=2 * seq * (2 * seq * width + 4 * width * local + 2 * seq * local),
            )
        )
    pooled, joined_low, qkv, stats, logs, context_low, attn_part = zip(*front)
    mid = []
    for row in rows:
        mid.append(
            run_kernel(
                mid_kernel,
                "mid",
                (
                    ((seq, width), f32),
                    ((seq, 1), f32),
                    ((seq, width), bf16),
                    ((seq, units), bf16),
                    ((seq, units), bf16),
                    ((seq, width), f32),
                ),
                (
                    (hidden,),
                    pooled[row],
                    attn_part[row],
                    [swap_cores(attn_part[row])],
                    out_biases,
                    norm_gains,
                    norm_biases,
                    [w_up],
                    up_bias_row,
                    [w_down],
                ),
                (),
                row,
                flops=4 * seq * width * units,
            )
        )
    normed, inv_std, first_low, act_low, slope, down_part = zip(*mid)
    turn = []
    for row in rows:
        turn.append(
            run_kernel(
                functools.partial(turn_kernel, row),
                "turn",
                (((seq, width), bf16), ((seq, width), f32), ((seq, width), bf16), ((8, width), f32)),
                (
                    normed[row],
                    down_part[row],
                    [swap_cores(down_part[row])],
                    (cotangent,),
                    out_biases,
                    norm_gains,
                    norm_biases,
                ),
                (lengths,),
                row,
                room=11,
                flops=seq * width,
            )
        )
    layer_out, d_down, d_down_low, turn_sums = zip(*turn)
    scattered = spread == 16 and width % 128 == 0
    token = lengths
    if scattered:
        here = lax.axis_index("dp").astype(jnp.int32).reshape(1)
        third = units // 3
        unit_cols = ((0, third), (third, third), (2 * third, third))
        twelfth = units // 12
        down_cols = ((0, 5 * twelfth), (5 * twelfth, 4 * twelfth), (9 * twelfth, 3 * twelfth))
        third = 4 * local // 3
        qkv_cols = ((0, third), (third, third), (2 * third, 3 * local - 2 * third))
        out_cols = ((0, 0), (0, 0), (0, local))
        down_blocks = grad_blocks(here, [list(zip(d_down_low, act_low))], [down_cols])
        down_sum, token = scatter_start(down_blocks, token)
    ffn_back = run_kernel(
        functools.partial(units_kernel, row_count),
        "units",
        (((seq, units), bf16), ((1, units), f32)) * row_count + (((row_count, seq, width), f32),),
        (w_down, w_up, *[array for pair in zip(d_down_low, slope) for array in pair]),
        (token,),
        flops=4 * row_count * seq * width * units,
    )
    d_up_low, up_sums, back_part = ffn_back[0:-1:2], ffn_back[1:-1:2], ffn_back[-1]
    if scattered:
        token = scatter_next(down_sum, token, up_sums)
        here, back_part, token = lax.optimization_barrier((here, back_part, token))
    back_other = swap_cores(back_part)
    if scattered:
        up_blocks = grad_blocks(here, [list(zip(first_low, d_up_low))], [unit_cols])
        up_blocks, back_other, token = lax.optimization_barrier((up_blocks, back_other, token))
        token = scatter_next(down_sum, token)
        token = scatter_next(down_sum, token)
        up_sum, token = scatter_start(up_blocks, token)
    back = run_kernel(
        functools.partial(back_kernel, row_count),
        "back",
        (
            ((seq, width), f32),
            ((seq, width), bf16),
            ((seq, 3 * local), bf16),
            ((8, width), f32),
            ((2, local), f32),
            ((seq, local), bf16),
        )
        * row_count
        + (((row_count, seq, width), f32),),
        (
            back_part,
            [back_other],
            norm_gains,
            [w_out],
            [w_parts],
            *[array for row in zip(d_down, normed, inv_std, qkv, logs) for array in row],
        ),
        (token,),
        flops=2 * row_count * seq * (4 * width * local + 5 * seq * local),
    )
    d_attn, d_attn_low, d_proj, back_sums, qv_sums = [back[index:-1:6] for index in range(5)]
    join_part = back[-1]
    if scattered:
        token = scatter_receive(down_sum, token, back_sums)
        token = scatter_next(up_sum, token)
        join_part, here, token = lax.optimization_barrier((join_part, here, token))
    join_other = swap_cores(join_part)
    if scattered:
        rest_blocks = grad_blocks(
            here, [list(zip(joined_low, d_proj)), list(zip(d_attn_low, context_low))], [qkv_cols, out_cols]
        )
        rest_blocks, token = lax.optimization_barrier((rest_blocks, token))
        token = scatter_receive(up_sum, token)
        rest_sum, token = scatter_start(rest_blocks, token)
    grad_inputs, join_grads = run_kernel(
        functools.partial(join_back_kernel, row_count, heads),
        "join_back",
        (((row_count, seq, width), f32), ((row_count, width), f32)),
        (
            hidden,
            spans,
            query_row,
            join_part,
            [join_other],
            *[array for row in zip(d_attn, pooled, stats) for array in row],
        ),
        (token,),
        flops=4 * row_count * seq * seq * width,
        room=17,
    )
    join_grad = jnp.sum(join_grads, 0)
    turn_sum = sum(turn_sums[1:], turn_sums[0])
    back_sum = sum(back_sums[1:], back_sums[0])
    small = (
        sum(qv_sums[1:], qv_sums[0]),
        sum(up_sums[1:], up_sums[0]).reshape(units),
        jnp.stack([back_sum[2], turn_sum[2]]),
        jnp.stack([back_sum[0], turn_sum[0]]),
        jnp.stack([back_sum[1], turn_sum[1]]),
        join_grad.reshape(width),
    )
    if scattered:
        sizes = [math.prod(value.shape) for value in small]
        room = SMALL_ROWS * rest_sum["widths"][0] - sum(sizes)
        assert room >= 0
        packed = jnp.concatenate([value.reshape(-1) for value in small] + [jnp.zeros((room,), f32)])
        packed = sum_step(packed.reshape(SMALL_ROWS, -1), STEP_X, token)
        (down_rows,) = scatter_result(down_sum, [[0, 1, 2]])
        token = scatter_send(up_sum, token)
        token = scatter_receive(up_sum, token, join_grad, down_rows)
        token = scatter_next(rest_sum, token, small=packed.reshape(1, SMALL_ROWS, -1))
        token = scatter_send(up_sum, token)
        token = scatter_next(rest_sum, token)
        token = scatter_next(rest_sum, token)
        token = scatter_receive(up_sum, token)
        (up_rows,) = scatter_result(up_sum, [[0, 1, 2]])
        token = scatter_receive(rest_sum, token, up_rows)
        first = 3 * local - 2 * third
        qkv_rows, out_rows, packed = scatter_result(
            rest_sum, [[(0, 0, third), (1, 0, third), (2, 0, first)], [(2, first, local)]]
        )
        qkv_rows = qkv_rows.reshape(-1, 3, local)
        packed = packed.reshape(-1)
        summed, offset = [], 0
        for value, size in zip(small, sizes):
            summed.append(packed[offset : offset + size].reshape(value.shape))
            offset += size
    else:

        def first_product(lefts, rights):
            total = sum(dot(left, right, TN) for left, right in zip(lefts, rights))
            return lax.psum_scatter(total, "dp", scatter_dimension=0, tiled=True)

        down_rows = first_product(d_down_low, act_low)
        up_rows = first_product(first_low, d_up_low)
        out_rows = first_product(d_attn_low, context_low)
        qkv_rows = first_product(joined_low, d_proj).reshape(-1, 3, local)
        summed = lax.psum(small, "dp")
    return (
        jnp.stack(layer_out),
        grad_inputs,
        qkv_rows,
        summed[0],
        out_rows,
        summed[2],
        summed[3],
        summed[4],
        up_rows,
        summed[1],
        down_rows,
        summed[5],
    )


def solution(mesh):
    return jax.shard_map(
        functools.partial(per_device, mesh.shape["dp"]),
        mesh=mesh,
        in_specs=(
            P("dp", None, None),
            P("dp"),
            P("dp", None),
            P(),
            P(None, None, "tensor"),
            P(None, "tensor"),
            P(None, "tensor"),
            P(),
            P(),
            P(),
            P(None, "tensor"),
            P("tensor"),
            P(None, "tensor"),
            P("dp", None, None),
        ),
        out_specs=(
            P("dp", None, None),
            P("dp", None, None),
            P("dp", None, "tensor"),
            P(None, "tensor"),
            P("dp", "tensor"),
            P(),
            P(),
            P(),
            P("dp", "tensor"),
            P("tensor"),
            P("dp", "tensor"),
            P(),
        ),
        check_vma=False,
    )
```

```python
import functools
import math

import jax
import jax.numpy as jnp
from jax import lax
from jax.experimental import pallas as pl
from jax.experimental.pallas import tpu as pltpu
from jax.sharding import PartitionSpec as P

HEAD = 64


EPS = 1e-05
NEGATIVE = -1e30
MEGA = 1024 * 1024
SMALL = 64 * 1024
SMALL_ROWS = 16


def swap_cores(part):
    return lax.ppermute(part, "tensor", [(0, 1), (1, 0)])


STEP_X, STEP_Y, STEP_Z, STEP_W = 1, 2, 4, 12
ORDERS = (
    (STEP_X, STEP_Y, STEP_Z, STEP_W),
    (STEP_Y, STEP_Z, STEP_X, STEP_W),
    (STEP_Z, STEP_X, STEP_Y, STEP_W),
)


def relative_block(order, place):
    steps = len(order)
    block = 0
    for position, mask in enumerate(order):
        if (place >> (steps - 1 - position)) & 1:
            block ^= mask
    return block


def dot(left, right, contract=((1,), (0,))):
    return lax.dot_general(left, right, (contract, ((), ())), preferred_element_type=jnp.float32)


NT = ((1,), (1,))
TN = ((0,), (0,))


class Arriving:
    def __init__(self, source, place, sem):
        self.copy, self.place, self.shape, self.waited = pltpu.make_async_copy(source, place, sem), place, place.shape, False
        self.copy.start()

    def ready(self):
        if not self.waited:
            self.copy.wait()
            self.waited = True
        return self.place

    def __getitem__(self, index):
        return self.ready()[index]


class Leaving:
    def __init__(self, place, target, sem):
        self.place, self.target, self.sem, self.shape, self.copies = place, target, sem, place.shape, []

    def __getitem__(self, index):
        return self.place[index]

    def __setitem__(self, index, value):
        self.place[index] = value

    def send(self, rows=slice(None), columns=slice(None)):
        source, target = self.place.at[rows, columns], self.target.at[rows, columns]
        self.copies.append(pltpu.make_async_copy(source, target, self.sem))
        self.copies[-1].start()

    def finish(self):
        if not self.copies:
            self.send()
        for copy in self.copies:
            copy.wait()


def moving_kernel(body, row, flags, scalar_count, *refs):
    count = len(flags)
    scalars, arrays, rest = refs[:scalar_count], refs[scalar_count : scalar_count + count], list(refs[scalar_count + count :])
    sems = rest.pop()
    views, leaving = [], []
    for index, (flag, array) in enumerate(zip(flags, arrays)):
        if flag == "small":
            views.append(array)
        elif flag == "out":
            views.append(Leaving(rest.pop(0), array, sems.at[index]))
            leaving.append(views[-1])
        else:
            source = array.at[row] if flag == "row" else array
            views.append(Arriving(source, rest.pop(0), sems.at[index]))
    body(*scalars, *views)
    for view in views:
        if isinstance(view, Arriving):
            view.ready()
    for view in leaving:
        view.finish()


def in_hbm(array):
    return pltpu.with_memory_space_constraint(array, pltpu.HBM)


def in_vmem(array):
    return pltpu.with_memory_space_constraint(array, pltpu.VMEM)


def run_kernel(body, name, outputs, operands, scalars=(), row=None, flops=0, room=12):
    flags, arrays, places, specs = [], [], [], []
    small_spec, large_spec = pl.BlockSpec(memory_space=pltpu.VMEM), pl.BlockSpec(memory_space=pltpu.HBM)
    for operand in operands:
        by_row, placed = isinstance(operand, tuple), isinstance(operand, list)
        array = operand[0] if by_row or placed else operand
        small = placed or array.size < SMALL
        arrays.append(in_vmem(array) if placed else array if small else in_hbm(array))
        flags.append("small" if small else "row" if by_row else "whole")
        specs.append(small_spec if small else large_spec)
        if not small:
            places.append(pltpu.VMEM(array.shape[1:] if by_row else array.shape, array.dtype))
    out_specs, out_shapes = [], []
    for shape, dtype in outputs:
        small = math.prod(shape) < SMALL
        flags.append("small" if small else "out")
        out_specs.append(small_spec if small else large_spec)
        out_shapes.append(jax.ShapeDtypeStruct(shape, dtype) if small else pltpu.HBM(shape, dtype))
        if not small:
            places.append(pltpu.VMEM(shape, dtype))
    held = sum(math.prod(place.shape) * jnp.dtype(place.dtype).itemsize for place in places)
    return pl.pallas_call(
        functools.partial(moving_kernel, body, row, flags, len(scalars)),
        out_shape=tuple(out_shapes),
        in_specs=[pl.BlockSpec(memory_space=pltpu.SMEM)] * len(scalars) + specs,
        out_specs=tuple(out_specs),
        scratch_shapes=places + [pltpu.SemaphoreType.DMA((len(flags),))],
        compiler_params=pltpu.CompilerParams(vmem_limit_bytes=held + room * MEGA),
        cost_estimate=pl.CostEstimate(flops=flops, bytes_accessed=held, transcendentals=0),
        name=name,
    )(*scalars, *arrays)


def square_iota(size):
    return lax.broadcasted_iota(jnp.int32, (size, size), 0), lax.broadcasted_iota(jnp.int32, (size, size), 1)


def halves(values):
    high = values.astype(jnp.bfloat16)
    return high, (values - high.astype(jnp.float32)).astype(jnp.bfloat16)


def same_span(spans_ref, row):
    span_row = spans_ref[row : row + 1, :].astype(jnp.float32)
    down, along = square_iota(span_row.shape[1])
    eye = down == along
    span_col = jnp.sum(jnp.where(eye, span_row, 0.0), 1, keepdims=True)
    return span_col == span_row, eye


def head_masks():
    lane = lax.broadcasted_iota(jnp.int32, (1, 2 * HEAD), 1)
    first = (lane < HEAD).astype(jnp.float32).astype(jnp.bfloat16)
    second = (lane >= HEAD).astype(jnp.float32).astype(jnp.bfloat16)
    return first, second


def pair_lanes(pair, start):
    return pl.ds(pl.multiple_of(start + pair * 2 * HEAD, 2 * HEAD), 2 * HEAD)


def norm_rows(resid):
    centered = resid - jnp.mean(resid, -1, keepdims=True)
    inv_std = lax.rsqrt(jnp.mean(centered * centered, -1, keepdims=True) + EPS)
    return centered * inv_std, inv_std


def norm_back(grad_in, gain_vec, normed, inv_std):
    d_normed = grad_in * gain_vec
    return inv_std * (
        d_normed
        - jnp.mean(d_normed, -1, keepdims=True)
        - normed * jnp.mean(d_normed * normed, -1, keepdims=True)
    )


def front_kernel(row, lengths_ref, hidden_ref, spans_ref, query_ref, w_qkv_ref, bias_ref, w_out_ref, *outs):
    pooled_ref, low_ref, qkv_ref, stats_ref, logs_ref, context_ref, part_ref = outs
    hidden = hidden_ref[row]
    seq, width = hidden.shape
    local = context_ref.shape[1]
    heads = local // HEAD
    inputs = hidden.astype(jnp.float32)
    score = jnp.sum(inputs * query_ref[...], 1, keepdims=True)
    same, eye = same_span(spans_ref, row)
    score_row = jnp.sum(jnp.where(eye, score, 0.0), 0, keepdims=True)
    top_row = jnp.max(jnp.where(same, score, NEGATIVE), 0, keepdims=True)
    weight_row = jnp.exp(score_row - top_row)
    weight = jnp.sum(jnp.where(eye, weight_row, 0.0), 1, keepdims=True)
    spread = jnp.where(same, weight_row, 0.0)
    total = jnp.sum(spread, 1, keepdims=True)
    high, low = halves(spread)
    pooled = (dot(high, hidden) + dot(low, hidden)) / total
    pooled_ref[...] = pooled
    pooled_ref.send()
    low_ref[...] = (inputs + pooled).astype(jnp.bfloat16)
    low_ref.send()
    lane = lax.broadcasted_iota(jnp.int32, (1, 128), 1)
    stats_ref[...] = jnp.where(lane == heads, total, jnp.where(lane == heads + 1, weight, 0.0))
    for part in range(3):
        columns = slice(part * local, (part + 1) * local)
        proj = dot(low_ref[...], w_qkv_ref[part]) + bias_ref[:, columns]
        if part == 0:
            proj = proj * (1.0 / math.sqrt(HEAD))
        qkv_ref[:, columns] = proj.astype(jnp.bfloat16)
    qkv_ref.send()
    valid = lax.broadcasted_iota(jnp.int32, (1, seq), 1) < lengths_ref[row]
    masks = head_masks()
    block = seq // 2

    def attend(pair, carry):
        query = qkv_ref[:, pair_lanes(pair, 0)]
        key = qkv_ref[:, pair_lanes(pair, local)]
        value = qkv_ref[:, pair_lanes(pair, 2 * local)]
        for step in range(2):
            rows = slice(step * block, (step + 1) * block)
            context = None
            stats = stats_ref[rows, :]
            for half in range(2):
                scores = dot(query[rows] * masks[half], key, NT)
                scores = jnp.where(valid, scores, NEGATIVE)
                top = jnp.max(scores, -1, keepdims=True)
                expo = jnp.exp(scores - top)
                expo_sum = jnp.sum(expo, -1, keepdims=True)
                probs = (expo * (1.0 / expo_sum)).astype(jnp.bfloat16)
                piece = dot(probs, value * masks[half])
                context = piece if context is None else context + piece
                stats = jnp.where(lane == 2 * pair + half, top + jnp.log(expo_sum), stats)
            stats_ref[rows, :] = stats
            context_ref[rows, pair_lanes(pair, 0)] = context.astype(jnp.bfloat16)
        return carry

    lax.fori_loop(0, heads // 2, attend, 0)
    context_ref.send()
    logs_ref[...] = jnp.transpose(stats_ref[...])[: logs_ref.shape[0]]
    for rows in (slice(0, block), slice(block, seq)):
        part_ref[rows, :] = dot(context_ref[rows, :], w_out_ref[...], NT)
        part_ref.send(rows=rows)


def mid_kernel(row, hidden_ref, pooled_ref, part_ref, other_ref, biases_ref, gains_ref, shifts_ref, w_up_ref, up_bias_ref, w_down_ref, *outs):
    normed_ref, inv_ref, low_ref, act_ref, slope_ref, down_ref = outs
    resid = hidden_ref[row].astype(jnp.float32) + pooled_ref[...]
    resid = resid + ((part_ref[...] + other_ref[...]) + biases_ref[0:1, :])
    normed, inv_std = norm_rows(resid)
    normed_ref[...] = normed
    normed_ref.send()
    inv_ref[...] = inv_std
    low_ref[...] = (normed * gains_ref[0:1, :] + shifts_ref[0:1, :]).astype(jnp.bfloat16)
    low_ref.send()
    chunk, step = 256, 64
    total = None
    for start in range(0, act_ref.shape[1], chunk):
        columns = slice(start, start + chunk)
        up = dot(low_ref[...], w_up_ref[:, columns]) + up_bias_ref[:, columns]
        for first in range(0, up.shape[0], step):
            rows = slice(first, first + step)
            piece = up[rows]
            cdf = 0.5 * (1.0 + lax.erf(piece * math.sqrt(0.5)))
            density = jnp.exp(piece * piece * -0.5) * (1.0 / math.sqrt(2.0 * math.pi))
            act_ref[rows, columns] = (piece * cdf).astype(jnp.bfloat16)
            slope_ref[rows, columns] = (cdf + piece * density).astype(jnp.bfloat16)
        down = dot(act_ref[:, columns], w_down_ref[:, columns], NT)
        total = down if total is None else total + down
        if start % (2 * chunk):
            act_ref.send(columns=slice(start - chunk, start + chunk))
            slope_ref.send(columns=slice(start - chunk, start + chunk))
    down_ref[...] = total


def turn_kernel(row, lengths_ref, normed_ref, down_ref, other_ref, cotangent_ref, biases_ref, gains_ref, shifts_ref, *outs):
    out_ref, d_down_ref, d_down_low_ref, sums_ref = outs
    seq = normed_ref.shape[0]
    first_norm = normed_ref[...] * gains_ref[0:1, :] + shifts_ref[0:1, :]
    normed, inv_std = norm_rows(first_norm + ((down_ref[...] + other_ref[...]) + biases_ref[1:2, :]))
    out_ref[...] = (normed * gains_ref[1:2, :] + shifts_ref[1:2, :]).astype(jnp.bfloat16)
    valid = (lax.broadcasted_iota(jnp.int32, (seq, 1), 0) < lengths_ref[row]).astype(jnp.float32)
    out_ref.send()
    d_out = cotangent_ref[...].astype(jnp.float32) * valid
    sums_ref[0:1, :] = jnp.sum(d_out * normed, 0, keepdims=True)
    sums_ref[1:2, :] = jnp.sum(d_out, 0, keepdims=True)
    d_down = norm_back(d_out, gains_ref[1:2, :], normed, inv_std)
    sums_ref[2:3, :] = jnp.sum(d_down, 0, keepdims=True)
    sums_ref[3:8, :] = jnp.zeros((5, sums_ref.shape[1]), jnp.float32)
    d_down_ref[...] = d_down
    d_down_low_ref[...] = d_down.astype(jnp.bfloat16)


def units_kernel(rows, token_ref, w_down_ref, w_up_ref, *refs):
    for row in range(rows):
        d_down_low_ref, slope_ref = refs[2 * row : 2 * row + 2]
        d_up_ref, up_sums_ref = refs[2 * rows + 2 * row : 2 * rows + 2 + 2 * row]
        back_ref = refs[4 * rows]
        chunk = 256
        total = None
        for start in range(0, d_up_ref.shape[1], chunk):
            columns = slice(start, start + chunk)
            d_up = dot(d_down_low_ref[...], w_down_ref[:, columns]) * slope_ref[:, columns].astype(jnp.float32)
            up_sums_ref[:, columns] = jnp.sum(d_up, 0, keepdims=True)
            d_up_ref[:, columns] = d_up.astype(jnp.bfloat16)
            back = dot(d_up_ref[:, columns], w_up_ref[:, columns], NT)
            total = back if total is None else total + back
            if start % (2 * chunk):
                d_up_ref.send(columns=slice(start - chunk, start + chunk))
        back_ref[row] = total
        back_ref.send(row)


def back_kernel(rows, lengths_ref, back_ref, other_ref, gains_ref, w_out_ref, w_qkv_ref, *refs):
    for row in range(rows):
        operands = refs[5 * row : 5 * row + 5]
        outs = refs[5 * rows + 6 * row : 5 * rows + 6 * row + 6]
        back_row(row, lengths_ref, back_ref, other_ref, gains_ref, w_out_ref, w_qkv_ref, *operands, *outs, refs[-1])


def back_row(row, lengths_ref, back_ref, other_ref, gains_ref, w_out_ref, w_qkv_ref, *refs):
    d_down_ref, normed_ref, inv_ref, qkv_ref, logs_ref = refs[:5]
    d_attn_ref, d_attn_low_ref, d_proj_ref, sums_ref, qv_sums_ref, d_context_ref, join_ref = refs[5:]
    seq = normed_ref.shape[0]
    local = d_context_ref.shape[1]
    normed = normed_ref[...]
    d_first = (back_ref[row] + other_ref[row]) + d_down_ref[...]
    sums_ref[0:1, :] = jnp.sum(d_first * normed, 0, keepdims=True)
    sums_ref[1:2, :] = jnp.sum(d_first, 0, keepdims=True)
    d_attn = norm_back(d_first, gains_ref[0:1, :], normed, inv_ref[...])
    sums_ref[2:3, :] = jnp.sum(d_attn, 0, keepdims=True)
    sums_ref[3:8, :] = jnp.zeros((5, sums_ref.shape[1]), jnp.float32)
    d_attn_ref[...] = d_attn
    d_attn_ref.send()
    d_attn_low_ref[...] = d_attn.astype(jnp.bfloat16)
    d_attn_low_ref.send()
    d_context_ref[...] = dot(d_attn_low_ref[...], w_out_ref[...]).astype(jnp.bfloat16)
    qkv_ref.ready()
    scale = 1.0 / math.sqrt(HEAD)
    masks = head_masks()
    block = seq // 2
    valid = lax.broadcasted_iota(jnp.int32, (seq, 1), 0) < lengths_ref[row]

    def attend(pair, carry):
        query = qkv_ref[:, pair_lanes(pair, 0)]
        key = qkv_ref[:, pair_lanes(pair, local)]
        value = qkv_ref[:, pair_lanes(pair, 2 * local)]
        grad = d_context_ref[:, pair_lanes(pair, 0)]
        d_key = d_value = None
        query_sum = jnp.zeros((1, 2 * HEAD), jnp.float32)
        for step in range(2):
            columns = slice(step * block, (step + 1) * block)
            d_query = None
            for half in range(2):
                query_part = query[columns] * masks[half]
                grad_part = grad[columns] * masks[half]
                scores = jnp.where(valid, dot(key, query_part, NT), NEGATIVE)
                probs = jnp.exp(scores - logs_ref[pl.ds(2 * pair + half, 1), columns])
                d_probs = dot(value, grad_part, NT)
                piece = dot(probs.astype(jnp.bfloat16), grad_part)
                d_value = piece if d_value is None else d_value + piece
                d_scores = probs * (d_probs - jnp.sum(d_probs * probs, 0, keepdims=True))
                d_scores = d_scores.astype(jnp.bfloat16)
                piece = dot(d_scores, query_part)
                d_key = piece if d_key is None else d_key + piece
                piece = dot(d_scores, key * masks[half], TN)
                d_query = piece if d_query is None else d_query + piece
            d_query = d_query * scale
            query_sum = query_sum + jnp.sum(d_query, 0, keepdims=True)
            d_proj_ref[columns, pair_lanes(pair, 0)] = d_query.astype(jnp.bfloat16)
        d_proj_ref[:, pair_lanes(pair, local)] = d_key.astype(jnp.bfloat16)
        d_proj_ref[:, pair_lanes(pair, 2 * local)] = d_value.astype(jnp.bfloat16)
        qv_sums_ref[0:1, pair_lanes(pair, 0)] = query_sum
        qv_sums_ref[1:2, pair_lanes(pair, 0)] = jnp.sum(d_value, 0, keepdims=True)
        return carry

    lax.fori_loop(0, local // (2 * HEAD), attend, 0)
    d_proj_ref.send()
    total = None
    for part in range(3):
        piece = dot(d_proj_ref[:, part * local : (part + 1) * local], w_qkv_ref[part], NT)
        total = piece if total is None else total + piece
    join_ref[row] = total
    join_ref.send(row)


def join_back_kernel(rows, heads, lengths_ref, hidden_ref, spans_ref, query_ref, join_ref, other_ref, *refs):
    grad_ref, sums_ref = refs[3 * rows :]
    for row in range(rows):
        join_back_row(row, heads, hidden_ref, spans_ref, query_ref, join_ref, other_ref, *refs[3 * row : 3 * row + 3], grad_ref, sums_ref)


def join_back_row(row, heads, hidden_ref, spans_ref, query_ref, join_ref, other_ref, d_attn_ref, pooled_ref, stats_ref, grad_ref, sums_ref):
    total = stats_ref[:, heads : heads + 1]
    weight = stats_ref[:, heads + 1 : heads + 2]
    d_joined = (join_ref[row] + other_ref[row]) + d_attn_ref[...]
    d_total = -jnp.sum(d_joined * pooled_ref[...], 1, keepdims=True) / total
    same, eye = same_span(spans_ref, row)
    d_total_row = jnp.sum(jnp.where(eye, d_total, 0.0), 0, keepdims=True)
    high, low = halves(d_joined / total)
    chosen = same.astype(jnp.float32).astype(jnp.bfloat16)
    d_weighted = dot(chosen, high) + dot(chosen, low)
    inputs = hidden_ref[row].astype(jnp.float32)
    d_weight = jnp.sum(jnp.where(same, d_total_row, 0.0), 1, keepdims=True)
    d_weight = d_weight + jnp.sum(d_weighted * inputs, 1, keepdims=True)
    d_score = weight * d_weight
    grad_ref[row] = d_joined + weight * d_weighted + d_score * query_ref[...]
    grad_ref.send(row)
    sums_ref[row : row + 1, :] = jnp.sum(d_score * inputs, 0, keepdims=True)


def grad_kernel(parts, rows, *refs):
    here_ref = refs[0]
    count = sum(2 * terms for _, terms in parts)
    sources = refs[1 : 1 + count]
    outs = refs[1 + count : 7 + count]
    places = refs[7 + count : 7 + 2 * count]
    turned = refs[7 + 2 * count : 7 + 2 * count + len(parts)]
    totals = refs[7 + 2 * count + len(parts) : -2]
    in_sems, sem = refs[-2:]
    here = here_ref[0]
    order_in = list(range(0, count, 2)) + list(range(1, count, 2))
    operands = {index: Arriving(sources[index], places[index], in_sems.at[index]) for index in order_in}
    copies = []
    first = 0
    for part, (_, terms) in enumerate(parts):
        for term in range(terms):
            left = operands[first + 2 * term]
            size = left.shape[0]
            turned[part][:, term * size : (term + 1) * size] = jnp.transpose(left[...])
        first += 2 * terms
    slot = 0
    for colour, order in enumerate(ORDERS):
        column = first = 0
        for part, (ranges, terms) in enumerate(parts):
            start, width = ranges[colour]
            if width:
                total = totals[slot]
                slot += 1
                product = None
                for term in range(terms):
                    right = operands[first + 2 * term + 1]
                    size = right.shape[0]
                    left = turned[part][:, term * size : (term + 1) * size]
                    piece = dot(left, right[:, start : start + width])
                    product = piece if product is None else product + piece
                total[...] = product
                for place in range(16):
                    block = jnp.bitwise_xor(here, relative_block(order, place))
                    source = total.at[pl.ds(pl.multiple_of(block * rows, 8), rows), :]
                    target = outs[2 * colour + place // 8].at[place % 8, :, pl.ds(column, width)]
                    copy = pltpu.make_async_copy(source, target, sem.at[colour])
                    copy.start()
                    copies.append(copy)
                column += width
            first += 2 * terms
    for copy in copies:
        copy.wait()


def grad_blocks(here, operands, parts):
    height = operands[0][0][0].shape[1]
    rows = height // 16
    widths = [sum(ranges[colour][1] for ranges in parts) for colour in range(3)]
    out_shape = []
    for width in widths:
        out_shape += [pltpu.HBM((8, rows, width), jnp.float32)] * 2
    flat = [array for pairs in operands for pair in pairs for array in pair]
    scratch = [pltpu.VMEM(array.shape, array.dtype) for array in flat]
    scratch += [pltpu.VMEM((height, sum(left.shape[0] for left, _ in pairs)), jnp.bfloat16) for pairs in operands]
    for colour in range(3):
        for ranges in parts:
            if ranges[colour][1]:
                scratch.append(pltpu.VMEM((height, ranges[colour][1]), jnp.float32))
    flops = sum(2 * left.size * right.shape[1] for pairs in operands for left, right in pairs)
    moved = sum(2 * array.size for array in flat) + sum(4 * 16 * rows * width for width in widths)
    return pl.pallas_call(
        functools.partial(grad_kernel, [(ranges, len(pairs)) for ranges, pairs in zip(parts, operands)], rows),
        out_shape=tuple(out_shape),
        in_specs=[pl.BlockSpec(memory_space=pltpu.SMEM)] + [pl.BlockSpec(memory_space=pltpu.HBM)] * len(flat),
        out_specs=tuple([pl.BlockSpec(memory_space=pltpu.HBM)] * 6),
        scratch_shapes=scratch + [pltpu.SemaphoreType.DMA((len(flat),)), pltpu.SemaphoreType.DMA((3,))],
        compiler_params=pltpu.CompilerParams(vmem_limit_bytes=30 * MEGA),
        cost_estimate=pl.CostEstimate(flops=flops, bytes_accessed=moved, transcendentals=0),
        name="weight_grads",
    )(here, *[in_hbm(array) for array in flat])


def combine_kernel(low, count, source_count, plan, extra, *refs):
    sources = refs[:source_count]
    out_count = len(plan) + (1 if extra and not low else 0)
    outs = refs[source_count : source_count + out_count]
    places = list(refs[source_count + out_count : -2])
    in_sems, out_sems = refs[-2:]
    arriving, small = [], []
    for group in plan:
        for sums, width in group:
            for index, column in sums:
                place = places.pop(0)
                rows = place.shape[1]
                source = sources[index].at[pl.ds(low, count), pl.ds(0, rows), pl.ds(column, width)]
                arriving.append(Arriving(source, place, in_sems.at[len(arriving)]))
    for index, block, row in extra:
        place = places.pop(0)
        source = sources[index].at[block, pl.ds(row, place.shape[0]), pl.ds(0, place.shape[1])]
        small.append(Arriving(source, place, in_sems.at[len(arriving) + len(small)]))
    leaving = []
    small_total = None
    for group, out in zip(plan, outs):
        place = places.pop(0)
        column = 0
        for sums, width in group:
            total = None
            for _ in sums:
                piece = arriving.pop(0)[...]
                total = piece if total is None else total + piece
            place[:count, :rows, column : column + width] = total
            column += width
        if extra and small_total is None:
            for view in small:
                small_total = view[...] if small_total is None else small_total + view[...]
            high, wide = small_total.shape
            if place.shape[0] > count:
                place[count] = jnp.zeros(place.shape[1:], jnp.float32)
                place[count, :high, :wide] = small_total
            elif place.shape[1] > rows:
                place[0, rows:, :] = jnp.zeros((high, place.shape[2]), jnp.float32)
                place[0, rows:, :wide] = small_total
        leaving.append(Leaving(place, out, out_sems.at[len(leaving)]))
        leaving[-1].send()
    if out_count > len(plan):
        place = places.pop(0)
        place[...] = small_total
        leaving.append(Leaving(place, outs[-1], out_sems.at[len(leaving)]))
    for view in leaving:
        view.finish()


def combine(state, low, count, groups):
    arrays, plan = [], []

    def number(array):
        for index, other in enumerate(arrays):
            if other is array:
                return index
        arrays.append(array)
        return len(arrays) - 1

    for group in groups:
        plan.append([])
        for piece in group:
            colour, start, width = piece if isinstance(piece, tuple) else (piece, 0, state["widths"][piece])
            plan[-1].append(([(number(array), column + start) for array, column in state["terms"][colour]], width))
    extra = [(number(array), block, row) for array, block, row in state["extra"]]
    rows = state["rows"]
    places = [
        pltpu.VMEM((count, rows, width), jnp.float32) for group in plan for sums, width in group for _ in sums
    ]
    small_shape = (SMALL_ROWS, state["widths"][0])
    places += [pltpu.VMEM(small_shape, jnp.float32) for _ in extra]
    term_count = len(places)
    results = [(count, rows, sum(width for _, width in group)) for group in plan]
    if extra and not low:
        results.append(small_shape)
    elif extra and len(groups) > 1:
        results[0] = (count + 1, *results[0][1:])
    elif extra:
        results[0] = (count, rows + SMALL_ROWS, results[0][2])
    places += [pltpu.VMEM(shape, jnp.float32) for shape in results]
    return pl.pallas_call(
        functools.partial(combine_kernel, low, count, len(arrays), plan, extra),
        out_shape=tuple(pltpu.HBM(shape, jnp.float32) for shape in results),
        in_specs=[pl.BlockSpec(memory_space=pltpu.HBM)] * len(arrays),
        out_specs=tuple([pl.BlockSpec(memory_space=pltpu.HBM)] * len(results)),
        scratch_shapes=places
        + [pltpu.SemaphoreType.DMA((term_count,)), pltpu.SemaphoreType.DMA((len(results),))],
        compiler_params=pltpu.CompilerParams(vmem_limit_bytes=16 * MEGA),
        cost_estimate=pl.CostEstimate(flops=1, bytes_accessed=1, transcendentals=0),
        name="combine",
    )(*[in_hbm(array) for array in arrays])


def scatter_groups(step):
    groups = []
    for colour, order in enumerate(ORDERS):
        for group in groups:
            if step >= 2 and set(ORDERS[group[0]][:step]) == set(order[:step]) and ORDERS[group[0]][step:] == order[step:]:
                group.append(colour)
                break
        else:
            groups.append([colour])
    return groups


def scatter_start(blocks, token):
    keeps = [blocks[2 * colour] for colour in range(3)]
    sends = [blocks[2 * colour + 1] for colour in range(3)]
    state = {"terms": [[(keep, 0)] for keep in keeps], "widths": [keep.shape[2] for keep in keeps], "half": 8, "step": 0}
    state.update(sends=sends, extra=[], rows=keeps[0].shape[1])
    return state, scatter_send(state, token)


def scatter_send(state, token):
    sends, token = lax.optimization_barrier((list(state["sends"]), token))
    state["incoming"] = [
        lax.ppermute(send, "dp", [(i, i ^ ORDERS[colours[0]][state["step"]]) for i in range(16)])
        for send, colours in zip(sends, scatter_groups(state["step"]))
    ]
    return token


def scatter_receive(state, token, *done, small=None):
    incoming, token, _ = lax.optimization_barrier((state["incoming"], token, done))
    for array, colours in zip(incoming, scatter_groups(state["step"])):
        column = 0
        for colour in colours:
            state["terms"][colour].append((array, column))
            column += state["widths"][colour]
    if state["extra"] and state["step"]:
        merged = len(incoming) == 1
        state["extra"].append((incoming[0], 0 if merged else state["half"], state["rows"] if merged else 0))
    if small is not None:
        state["extra"] = [(small, 0, 0)]
    state["step"] += 1
    state["half"] //= 2
    if state["half"]:
        sends = combine(state, state["half"], state["half"], scatter_groups(state["step"]))
        state["sends"], token = lax.optimization_barrier((sends, token))
    return token


def scatter_next(state, token, *done, small=None):
    return scatter_send(state, scatter_receive(state, token, *done, small=small))


def scatter_result(state, groups):
    results = combine(state, 0, 1, groups)
    return [result[0] for result in results[: len(groups)]] + list(results[len(groups) :])


def sum_step(values, mask, token):
    values, token = lax.optimization_barrier((values, token))
    return values + lax.ppermute(values, "dp", [(i, i ^ mask) for i in range(16)])


def per_device(
    spread,
    hidden,
    lengths,
    spans,
    join_query,
    w_qkv,
    qv_bias,
    w_out,
    out_biases,
    norm_gains,
    norm_biases,
    w_up,
    up_bias,
    w_down,
    cotangent,
):
    row_count, seq, width = hidden.shape
    local = w_qkv.shape[2]
    units = w_up.shape[1]
    heads = local // HEAD
    rows = range(row_count)
    f32, bf16 = jnp.float32, jnp.bfloat16
    query_row = join_query.reshape(1, width)
    w_parts = jnp.transpose(w_qkv, (1, 0, 2))
    qkv_bias = jnp.concatenate([qv_bias[0], jnp.zeros((local,), f32), qv_bias[1]]).reshape(1, 3 * local)
    up_bias_row = up_bias.reshape(1, units)
    log_rows = 8 * (-(-heads // 8))

    front = []
    for row in rows:
        front.append(
            run_kernel(
                functools.partial(front_kernel, row),
                "front",
                (
                    ((seq, width), f32),
                    ((seq, width), bf16),
                    ((seq, 3 * local), bf16),
                    ((seq, 128), f32),
                    ((log_rows, seq), f32),
                    ((seq, local), bf16),
                    ((seq, width), f32),
                ),
                ([hidden], spans, query_row, [w_parts], qkv_bias, [w_out]),
                (lengths,),
                row,
                flops=2 * seq * (2 * seq * width + 4 * width * local + 2 * seq * local),
            )
        )
    pooled, joined_low, qkv, stats, logs, context_low, attn_part = zip(*front)
    mid = []
    for row in rows:
        mid.append(
            run_kernel(
                functools.partial(mid_kernel, row),
                "mid",
                (
                    ((seq, width), f32),
                    ((seq, 1), f32),
                    ((seq, width), bf16),
                    ((seq, units), bf16),
                    ((seq, units), bf16),
                    ((seq, width), f32),
                ),
                (
                    [hidden],
                    pooled[row],
                    attn_part[row],
                    [swap_cores(attn_part[row])],
                    out_biases,
                    norm_gains,
                    norm_biases,
                    [w_up],
                    up_bias_row,
                    [w_down],
                ),
                (),
                row,
                flops=4 * seq * width * units,
            )
        )
    normed, inv_std, first_low, act_low, slope, down_part = zip(*mid)
    turn = []
    for row in rows:
        turn.append(
            run_kernel(
                functools.partial(turn_kernel, row),
                "turn",
                (((seq, width), bf16), ((seq, width), f32), ((seq, width), bf16), ((8, width), f32)),
                (
                    normed[row],
                    down_part[row],
                    [swap_cores(down_part[row])],
                    (cotangent,),
                    out_biases,
                    norm_gains,
                    norm_biases,
                ),
                (lengths,),
                row,
                room=11,
                flops=seq * width,
            )
        )
    layer_out, d_down, d_down_low, turn_sums = zip(*turn)
    scattered = spread == 16 and width % 128 == 0
    token = lengths
    if scattered:
        here = lax.axis_index("dp").astype(jnp.int32).reshape(1)
        third = units // 3
        unit_cols = ((0, third), (third, third), (2 * third, third))
        twelfth = units // 12
        down_cols = ((0, 5 * twelfth), (5 * twelfth, 4 * twelfth), (9 * twelfth, 3 * twelfth))
        third = 4 * local // 3
        qkv_cols = ((0, third), (third, third), (2 * third, 3 * local - 2 * third))
        out_cols = ((0, 0), (0, 0), (0, local))
        down_blocks = grad_blocks(here, [list(zip(d_down_low, act_low))], [down_cols])
        down_sum, token = scatter_start(down_blocks, token)
    ffn_back = run_kernel(
        functools.partial(units_kernel, row_count),
        "units",
        (((seq, units), bf16), ((1, units), f32)) * row_count + (((row_count, seq, width), f32),),
        (w_down, w_up, *[array for pair in zip(d_down_low, slope) for array in pair]),
        (token,),
        flops=4 * row_count * seq * width * units,
    )
    d_up_low, up_sums, back_part = ffn_back[0:-1:2], ffn_back[1:-1:2], ffn_back[-1]
    if scattered:
        token = scatter_next(down_sum, token, up_sums)
        here, back_part, token = lax.optimization_barrier((here, back_part, token))
    back_other = swap_cores(back_part)
    if scattered:
        up_blocks = grad_blocks(here, [list(zip(first_low, d_up_low))], [unit_cols])
        up_blocks, back_other, token = lax.optimization_barrier((up_blocks, back_other, token))
        token = scatter_next(down_sum, token)
        token = scatter_next(down_sum, token)
        up_sum, token = scatter_start(up_blocks, token)
    back = run_kernel(
        functools.partial(back_kernel, row_count),
        "back",
        (
            ((seq, width), f32),
            ((seq, width), bf16),
            ((seq, 3 * local), bf16),
            ((8, width), f32),
            ((2, local), f32),
            ((seq, local), bf16),
        )
        * row_count
        + (((row_count, seq, width), f32),),
        (
            back_part,
            [back_other],
            norm_gains,
            [w_out],
            [w_parts],
            *[array for row in zip(d_down, normed, inv_std, qkv, logs) for array in row],
        ),
        (token,),
        flops=2 * row_count * seq * (4 * width * local + 5 * seq * local),
    )
    d_attn, d_attn_low, d_proj, back_sums, qv_sums = [back[index:-1:6] for index in range(5)]
    join_part = back[-1]
    if scattered:
        token = scatter_receive(down_sum, token, back_sums)
        token = scatter_next(up_sum, token)
        join_part, here, token = lax.optimization_barrier((join_part, here, token))
    join_other = swap_cores(join_part)
    if scattered:
        rest_blocks = grad_blocks(
            here, [list(zip(joined_low, d_proj)), list(zip(d_attn_low, context_low))], [qkv_cols, out_cols]
        )
        rest_blocks, token = lax.optimization_barrier((rest_blocks, token))
        token = scatter_receive(up_sum, token)
        rest_sum, token = scatter_start(rest_blocks, token)
    grad_inputs, join_grads = run_kernel(
        functools.partial(join_back_kernel, row_count, heads),
        "join_back",
        (((row_count, seq, width), f32), ((row_count, width), f32)),
        (
            hidden,
            spans,
            query_row,
            join_part,
            [join_other],
            *[array for row in zip(d_attn, pooled, stats) for array in row],
        ),
        (token,),
        flops=4 * row_count * seq * seq * width,
        room=17,
    )
    join_grad = jnp.sum(join_grads, 0)
    turn_sum = sum(turn_sums[1:], turn_sums[0])
    back_sum = sum(back_sums[1:], back_sums[0])
    small = (
        sum(qv_sums[1:], qv_sums[0]),
        sum(up_sums[1:], up_sums[0]).reshape(units),
        jnp.stack([back_sum[2], turn_sum[2]]),
        jnp.stack([back_sum[0], turn_sum[0]]),
        jnp.stack([back_sum[1], turn_sum[1]]),
        join_grad.reshape(width),
    )
    if scattered:
        sizes = [math.prod(value.shape) for value in small]
        room = SMALL_ROWS * rest_sum["widths"][0] - sum(sizes)
        assert room >= 0
        packed = jnp.concatenate([value.reshape(-1) for value in small] + [jnp.zeros((room,), f32)])
        packed = sum_step(packed.reshape(SMALL_ROWS, -1), STEP_X, token)
        (down_rows,) = scatter_result(down_sum, [[0, 1, 2]])
        token = scatter_send(up_sum, token)
        token = scatter_receive(up_sum, token, join_grad, down_rows)
        token = scatter_next(rest_sum, token, small=packed.reshape(1, SMALL_ROWS, -1))
        token = scatter_send(up_sum, token)
        token = scatter_next(rest_sum, token)
        token = scatter_next(rest_sum, token)
        token = scatter_receive(up_sum, token)
        (up_rows,) = scatter_result(up_sum, [[0, 1, 2]])
        token = scatter_receive(rest_sum, token, up_rows)
        first = 3 * local - 2 * third
        qkv_rows, out_rows, packed = scatter_result(
            rest_sum, [[(0, 0, third), (1, 0, third), (2, 0, first)], [(2, first, local)]]
        )
        qkv_rows = qkv_rows.reshape(-1, 3, local)
        packed = packed.reshape(-1)
        summed, offset = [], 0
        for value, size in zip(small, sizes):
            summed.append(packed[offset : offset + size].reshape(value.shape))
            offset += size
    else:

        def first_product(lefts, rights):
            total = sum(dot(left, right, TN) for left, right in zip(lefts, rights))
            return lax.psum_scatter(total, "dp", scatter_dimension=0, tiled=True)

        down_rows = first_product(d_down_low, act_low)
        up_rows = first_product(first_low, d_up_low)
        out_rows = first_product(d_attn_low, context_low)
        qkv_rows = first_product(joined_low, d_proj).reshape(-1, 3, local)
        summed = lax.psum(small, "dp")
    return (
        jnp.stack(layer_out),
        grad_inputs,
        qkv_rows,
        summed[0],
        out_rows,
        summed[2],
        summed[3],
        summed[4],
        up_rows,
        summed[1],
        down_rows,
        summed[5],
    )


def solution(mesh):
    return jax.shard_map(
        functools.partial(per_device, mesh.shape["dp"]),
        mesh=mesh,
        in_specs=(
            P("dp", None, None),
            P("dp"),
            P("dp", None),
            P(),
            P(None, None, "tensor"),
            P(None, "tensor"),
            P(None, "tensor"),
            P(),
            P(),
            P(),
            P(None, "tensor"),
            P("tensor"),
            P(None, "tensor"),
            P("dp", None, None),
        ),
        out_specs=(
            P("dp", None, None),
            P("dp", None, None),
            P("dp", None, "tensor"),
            P(None, "tensor"),
            P("dp", "tensor"),
            P(),
            P(),
            P(),
            P("dp", "tensor"),
            P("tensor"),
            P("dp", "tensor"),
            P(),
        ),
        check_vma=False,
    )
```
